32 devices in a mesh: exp: 8 (over z, y), hid: 4 (over x, core).
Axes of the slice: x: 2, y: 2, z: 4, core: 2. Of those that a mesh axis runs over, the one named last changes fastest.
Arguments:
- patches: bfloat16 [8192, 768], P(('exp', 'hid')), may hold values from -6 to 6
- cotangent: bfloat16 [8192, 768], P(('exp', 'hid')), may hold values from -6 to 6
- timesteps: int32 [32], P(('exp', 'hid')), may hold values from 0 to 999
- labels: int32 [32], P(('exp', 'hid')), may hold values from 0 to 1000
- routes: int32 [8192, 2], P(('exp', 'hid')), may hold values from 0 to 7, as said below
- slot_index: int32 [8192, 2], P(('exp', 'hid')), may hold values from 0 to 72, as said below
- time_weight: bfloat16 [256, 768], replicated, may hold values from -0.375 to 0.375
- time_bias: float32 [768], replicated, may hold values from -3 to 3
- class_table: bfloat16 [1001, 768], replicated, may hold values from -3 to 3
- ada_weight: bfloat16 [768, 4608], replicated, may hold values from -0.21875 to 0.21875
- ada_bias: float32 [4608], replicated, may hold values from -3 to 3
- qkv_weight: bfloat16 [768, 2304], replicated, may hold values from -0.21875 to 0.21875
- proj_weight: bfloat16 [768, 768], replicated, may hold values from -1.25 to 1.25
- router_weight: bfloat16 [768, 8], replicated, may hold values from -0.4375 to 0.4375
- shared_in: bfloat16 [768, 3072], P(None, 'hid'), may hold values from -0.21875 to 0.21875
- shared_out: bfloat16 [3072, 768], P('hid'), may hold values from -0.109375 to 0.109375
- expert_in: bfloat16 [8, 768, 3072], P('exp', None, 'hid'), may hold values from -0.21875 to 0.21875
- expert_out: bfloat16 [8, 3072, 768], P('exp', 'hid'), may hold values from -0.109375 to 0.109375
Outputs:
- output: bfloat16 [8192, 768], P(('exp', 'hid'))
- grad_patches: bfloat16 [8192, 768], P(('exp', 'hid'))
- grad_time_weight: float32 [256, 768], P('exp')
- grad_time_bias: float32 [768], replicated
- grad_class_table: float32 [1001, 768], replicated
- grad_ada_weight: float32 [768, 4608], P('exp')
- grad_ada_bias: float32 [4608], replicated
- grad_qkv_weight: float32 [768, 2304], P('exp')
- grad_proj_weight: float32 [768, 768], P('exp')
- grad_router_weight: float32 [768, 8], P('exp')
- grad_shared_in: float32 [768, 3072], P('exp', 'hid')
- grad_shared_out: float32 [3072, 768], P('hid', 'exp')
- grad_expert_in: float32 [8, 768, 3072], P('exp', None, 'hid')
- grad_expert_out: float32 [8, 3072, 768], P('exp', 'hid')
- expert_counts: float32 [8], replicated
The draws below stay inside these ranges and needn't reach their ends.
Inputs may be any that keep to these rules, and one draw needn't show every extreme that they name: `routes`: each patch names two different experts, its first and second choice. On every device the first 72 patches name the same expert first. `slot_index`: for each pair of a patch and a choice: the number of earlier pairs of the same device (patch order, first choice before second) that name the same expert, or 72 where that number is 72 or more (the pair is dropped).
All inputs are finite; a program needn't handle non-finite values.
Results may differ from the reference program's by a relative error of at most 0.028.
Values may be sent and summed in bfloat16 or wider, within the bound.
No kernel may reach another device: no remote copies, remote signals or barrier semaphores. Data moves between devices by JAX's collectives and lax.ppermute only.
A program may use at most 192 MiB of HBM per device.

```python
import math
from functools import partial
import jax
import jax.numpy as jnp
from jax import lax

D = 768
HEADS = 12
HDIM = 64
FF = 3072
FREQ = 256
CLASSES = 1001
SEQ = 256
TOK = 256
ITEMS = 32
TOKENS = 8192
EXPERTS = 8
CAP = 72
N_EXP = 8
N_HID = 4


def route_table(key):
    base = jax.random.fold_in(key, 11)
    key_perm, key_one, key_two, key_three, key_offset = jax.random.split(base, 5)
    order = jax.random.permutation(key_perm, EXPERTS)
    draw_one = jax.random.randint(key_one, (TOKENS,), 0, EXPERTS)
    draw_two = jax.random.randint(key_two, (TOKENS,), 0, EXPERTS)
    draw_three = jax.random.randint(key_three, (TOKENS,), 0, EXPERTS)
    ranked = jnp.minimum(jnp.minimum(draw_one, draw_two), draw_three)
    position = jnp.arange(TOKENS, dtype=jnp.int32) % TOK
    ranked = jnp.where(position < CAP, 0, ranked)
    first_choice = order[ranked]
    offsets = jax.random.randint(key_offset, (TOKENS,), 1, EXPERTS)
    second_choice = (first_choice + offsets) % EXPERTS
    return jnp.stack([first_choice, second_choice], axis=1).astype(jnp.int32)


def draw_routes(key, part):
    return route_table(key)


def draw_slot_index(key, part):
    table = route_table(key)
    blocks = TOKENS // TOK
    expert_hot = (table.reshape(blocks, 2 * TOK)[:, :, None] == jnp.arange(EXPERTS, dtype=jnp.int32)[None, None, :]).astype(jnp.int32)
    ranked = jnp.sum((jnp.cumsum(expert_hot, axis=1) - 1) * expert_hot, axis=2)
    return jnp.minimum(ranked, CAP).reshape(TOKENS, 2).astype(jnp.int32)


def plant(values, key, low, largest):
    dims = values.shape
    spot = [jax.random.randint(jax.random.fold_in(key, axis), (), 0, dims[axis]) for axis in range(len(dims))]
    values = values.at[tuple(spot)].set(low)
    longest = dims.index(max(dims))
    spot[longest] = (spot[longest] + 1) % dims[longest]
    return values.at[tuple(spot)].set(largest)


def shard_levels(rng, shape, cuts, least, top_value):
    gain = 1.0
    for dim, shards_of in cuts:
        draws = jax.random.uniform(jax.random.fold_in(jax.random.fold_in(rng, 6), dim), (shards_of,), jnp.float32, least / len(cuts), top_value / len(cuts))
        gain = gain * jnp.repeat(jnp.exp(draws), shape[dim] // shards_of).reshape((-1,) + (1,) * (len(shape) - 1 - dim))
    return gain


def scatter_about(stream_key, dims, deviation, reach, pieces=(), kind=jnp.bfloat16):
    entries = deviation * jax.random.normal(stream_key, dims, jnp.float32)
    if pieces:
        entries = entries * shard_levels(stream_key, dims, pieces, -0.22, 0.18)
    return jnp.clip(entries, -reach, reach).astype(kind)


def setup_inputs(seed: int = 0) -> dict:
    key_list = jax.random.split(jax.random.key(seed), 19)
    return {
        "patches": scatter_about(key_list[0], (TOKENS, D), 1.0, 6.0, ((0, 32),)),
        "cotangent": scatter_about(key_list[1], (TOKENS, D), 1.0, 6.0, ((0, 32),)),
        "timesteps": plant(jax.random.randint(key_list[2], (ITEMS,), 0, 1000), jax.random.fold_in(key_list[2], 1), 0, 999).astype(jnp.int32),
        "labels": plant(jax.random.randint(key_list[3], (ITEMS,), 0, CLASSES), jax.random.fold_in(key_list[3], 1), 0, CLASSES - 1).astype(jnp.int32),
        "routes": draw_routes(jax.random.fold_in(key_list[18], 71), 0),
        "slot_index": draw_slot_index(jax.random.fold_in(key_list[18], 71), 0),
        "time_weight": scatter_about(key_list[6], (FREQ, D), FREQ ** -0.5, 0.375),
        "time_bias": scatter_about(key_list[7], (D,), 0.5, 3.0, (), jnp.float32),
        "class_table": scatter_about(key_list[8], (CLASSES, D), 0.5, 3.0),
        "ada_weight": scatter_about(key_list[9], (D, 6 * D), D ** -0.5, 0.21875),
        "ada_bias": scatter_about(key_list[10], (6 * D,), 0.5, 3.0, (), jnp.float32),
        "qkv_weight": scatter_about(key_list[11], (D, 3 * D), D ** -0.5, 0.21875),
        "proj_weight": scatter_about(key_list[12], (D, D), (D // 32) ** -0.5, 1.25),
        "router_weight": scatter_about(key_list[13], (D, EXPERTS), (D // 4) ** -0.5, 0.4375),
        "shared_in": scatter_about(key_list[14], (D, FF), D ** -0.5, 0.21875, ((1, 4),)),
        "shared_out": scatter_about(key_list[15], (FF, D), FF ** -0.5, 0.109375, ((0, 4),)),
        "expert_in": scatter_about(key_list[16], (EXPERTS, D, FF), D ** -0.5, 0.21875, ((0, 8), (2, 4))),
        "expert_out": scatter_about(key_list[17], (EXPERTS, FF, D), FF ** -0.5, 0.109375, ((0, 8), (1, 4))),
    }


@jax.custom_vjp
def low(v):
    return lax.optimization_barrier(v.astype(jnp.bfloat16)).astype(jnp.float32)

@jax.custom_vjp
def low_back(v):
    return v

def low_keep(v):
    return (low(v), None)

def low_pass(kept, grad):
    return (grad,)

def back_keep(v):
    return (v, None)

def back_low(kept, grad):
    return (low(grad),)
low.defvjp(low_keep, low_pass)
low_back.defvjp(back_keep, back_low)
eps_norm = 1e-06
highest = lax.Precision.HIGHEST

def mat_high(left_side, right_side):
    return jnp.dot(left_side, right_side, precision=highest, preferred_element_type=jnp.float32)

def sinus_table(timesteps, columns):
    half_cols = columns // 2
    freqs = jnp.exp(-math.log(10000.0) * jnp.arange(half_cols, dtype=jnp.float32) / half_cols)
    angles = timesteps.astype(jnp.float32)[:, None] * freqs[None, :]
    return jnp.concatenate([jnp.cos(angles), jnp.sin(angles)], axis=1)

def normalize(inputs):
    center = inputs - lax.optimization_barrier(jnp.mean(inputs, axis=-1, keepdims=True))
    return center * lax.rsqrt(lax.optimization_barrier(jnp.mean(center * center, axis=-1, keepdims=True)) + eps_norm)

def attend_group(qkv_group):
    queries = qkv_group[:, :, 0]
    key_rows = qkv_group[:, :, 1]
    value_rows = qkv_group[:, :, 2]
    raw_scores = jnp.einsum('bqhd,bkhd->bhqk', queries, key_rows, precision=highest)
    scores = low_back(raw_scores) * (1.0 / math.sqrt(HDIM))
    shifted = jnp.exp(scores - lax.optimization_barrier(jnp.max(scores, axis=-1, keepdims=True)))
    attention = shifted / lax.optimization_barrier(jnp.sum(shifted, axis=-1, keepdims=True))
    return jnp.einsum('bhqk,bkhd->bqhd', low(attention), value_rows, precision=highest)

def expert_block(operands):
    rows_in, weight_in, weight_out = operands
    pre_act = low_back(mat_high(rows_in, weight_in))
    activated = low(jax.nn.gelu(pre_act))
    return low(low_back(mat_high(activated, weight_out)))

def forward(patches, time_weight, time_bias, class_table, ada_weight, ada_bias, qkv_weight, proj_weight, router_weight, shared_in, shared_out, expert_in, expert_out, timesteps, labels, routes, slot_index):
    devices = N_EXP * N_HID
    item_count = timesteps.shape[0]
    freq_emb = low(sinus_table(timesteps, FREQ))
    condition = low_back(mat_high(freq_emb, time_weight)) + time_bias + class_table[labels]
    modulate = low_back(mat_high(low(jax.nn.silu(condition)), ada_weight)) + ada_bias
    spans = modulate.reshape(item_count, 6, 1, D)
    shift_one, scale_one, gate_one = (spans[:, 0], spans[:, 1], spans[:, 2])
    shift_two, scale_two, gate_two = (spans[:, 3], spans[:, 4], spans[:, 5])
    residual = patches.reshape(item_count, SEQ, D)
    hidden_one = low(normalize(residual) * (1.0 + scale_one) + shift_one)
    qkv_rows = low(low_back(mat_high(hidden_one.reshape(TOKENS, D), qkv_weight)))
    group_items = math.gcd(item_count, max(1, 4096 // SEQ))
    qkv_groups = qkv_rows.reshape(item_count // group_items, group_items, SEQ, 3, HEADS, HDIM)
    attended = lax.map(jax.checkpoint(attend_group), qkv_groups).reshape(TOKENS, D)
    attended = low(low_back(attended))
    branch_one = low_back(mat_high(attended, proj_weight)).reshape(item_count, SEQ, D)
    residual_one = residual + gate_one * branch_one
    hidden_two = low(normalize(residual_one) * (1.0 + scale_two) + shift_two).reshape(TOKENS, D)
    logits = low_back(mat_high(hidden_two, router_weight))
    chosen = jnp.take_along_axis(logits, routes, axis=1)
    gate_first = jax.nn.sigmoid(chosen[:, 0] - chosen[:, 1])
    gate_pair = jnp.stack([gate_first, 1.0 - gate_first], axis=1)
    shared_pre = low_back(mat_high(hidden_two, shared_in))
    shared_sum = low_back(mat_high(low(jax.nn.gelu(shared_pre)), shared_out))
    device_rows = hidden_two.reshape(devices, TOK, D)
    device_ids = jnp.arange(devices, dtype=jnp.int32)[:, None, None]
    expert_ids = routes.reshape(devices, TOK, 2).astype(jnp.int32)
    slot_ids = slot_index.reshape(devices, TOK, 2).astype(jnp.int32)
    buffers = jnp.zeros((devices, EXPERTS, CAP + 1, D), jnp.float32)
    buffers = buffers.at[device_ids, expert_ids, slot_ids].add(jnp.broadcast_to(device_rows[:, :, None, :], (devices, TOK, 2, D)))
    buffers = low_back(buffers[:, :, :CAP])
    by_expert = jnp.transpose(buffers, (1, 0, 2, 3)).reshape(EXPERTS, devices * CAP, D)
    expert_rows = lax.map(jax.checkpoint(expert_block), (by_expert, expert_in, expert_out))
    expert_rows = jnp.transpose(expert_rows.reshape(EXPERTS, devices, CAP, D), (1, 0, 2, 3))
    padded = jnp.concatenate([expert_rows, jnp.zeros((devices, EXPERTS, 1, D), jnp.float32)], axis=2)
    picked = padded[device_ids, expert_ids, slot_ids]
    moe_out = lax.optimization_barrier(jnp.sum(gate_pair.reshape(devices, TOK, 2, 1) * picked, axis=2)).reshape(item_count, SEQ, D)
    result = residual_one + gate_two * (shared_sum.reshape(item_count, SEQ, D) + moe_out)
    return result.reshape(TOKENS, D)

def reference(patches, cotangent, timesteps, labels, routes, slot_index, time_weight, time_bias, class_table, ada_weight, ada_bias, qkv_weight, proj_weight, router_weight, shared_in, shared_out, expert_in, expert_out):
    floats = tuple((array_in.astype(jnp.float32) for array_in in (patches, time_weight, time_bias, class_table, ada_weight, ada_bias, qkv_weight, proj_weight, router_weight, shared_in, shared_out, expert_in, expert_out)))
    forward_fixed = partial(forward, timesteps=timesteps, labels=labels, routes=routes, slot_index=slot_index)
    result, pullback = jax.vjp(forward_fixed, *floats)
    gradients = pullback(cotangent.astype(jnp.float32))
    kept_pairs = (slot_index < CAP).astype(jnp.float32)
    expert_hot = (routes[:, :, None] == jnp.arange(EXPERTS, dtype=jnp.int32)[None, None, :]).astype(jnp.float32)
    expert_counts = lax.optimization_barrier(jnp.sum(expert_hot * kept_pairs[:, :, None], axis=(0, 1)))
    return (result.astype(jnp.bfloat16), gradients[0].astype(jnp.bfloat16), gradients[1], gradients[2], gradients[3], gradients[4], gradients[5], gradients[6], gradients[7], gradients[8], gradients[9], gradients[10], gradients[11], gradients[12], expert_counts)
```

```python
import math

import jax
import jax.numpy as jnp
from jax import lax
from jax.sharding import PartitionSpec as P

HEADS = 12
HDIM = 64
SEQ = 256


eps_norm = 1e-06
highest = lax.Precision.HIGHEST


def mat_prod(left_side, right_side):
    return jnp.dot(left_side, right_side, preferred_element_type=jnp.float32)


def prod_rows(left_side, right_side):
    return lax.dot_general(
        left_side, right_side, (((0,), (0,)), ((), ())), preferred_element_type=jnp.float32
    )


def prod_cols(left_side, right_side):
    return lax.dot_general(
        left_side, right_side, (((1,), (1,)), ((), ())), preferred_element_type=jnp.float32
    )


def sinus_table(timesteps, columns):
    half_cols = columns // 2
    freqs = jnp.exp(-math.log(10000.0) * jnp.arange(half_cols, dtype=jnp.float32) / half_cols)
    angles = timesteps.astype(jnp.float32)[:, None] * freqs[None, :]
    return jnp.concatenate([jnp.cos(angles), jnp.sin(angles)], axis=1)


def normalize(inputs):
    center = inputs - jnp.mean(inputs, axis=-1, keepdims=True)
    inverse = lax.rsqrt(jnp.mean(center * center, axis=-1, keepdims=True) + eps_norm)
    return (center * inverse, inverse)


def normalize_back(normed, inverse, grad_normed):
    return inverse * (
        grad_normed
        - jnp.mean(grad_normed, axis=-1, keepdims=True)
        - normed * jnp.mean(grad_normed * normed, axis=-1, keepdims=True)
    )


def gelu_back(pre_act, grad_act):
    return jax.vjp(jax.nn.gelu, pre_act)[1](grad_act)[0]


def attention_weights(queries, key_rows, score_scale):
    scores = (
        jnp.einsum("bqhd,bkhd->bhqk", queries, key_rows, preferred_element_type=jnp.float32)
        * score_scale
    )
    row_max = jnp.max(scores, axis=-1, keepdims=True)
    log_total = row_max + jnp.log(jnp.sum(jnp.exp(scores - row_max), axis=-1, keepdims=True))
    return jnp.exp(scores - log_total)


def pairs_of(size, mask):
    return [(index, index ^ mask) for index in range(size)]


def swap(values, axis, mask):
    return lax.ppermute(values, axis, pairs_of(lax.axis_size(axis), mask))


def low(values):
    return values.astype(jnp.bfloat16)


def bits_of(axis):
    masks = [1]
    while masks[-1] * 2 < lax.axis_size(axis):
        masks.append(masks[-1] * 2)
    return masks


def gather_hid(own):
    blocks = {0: own}
    for mask in reversed(bits_of("hid")):
        for index in list(blocks):
            blocks[index ^ mask] = swap(blocks[index], "hid", mask)
    return [blocks[index] for index in range(lax.axis_size("hid"))]


def reduce_hid(blocks):
    blocks = dict(enumerate(blocks))
    for mask in bits_of("hid"):
        moved = {
            index: swap(low(blocks[index | mask]), "hid", mask)
            for index in blocks
            if not index & mask
        }
        blocks = {
            index: blocks[index].astype(jnp.float32) + moved[index].astype(jnp.float32)
            for index in moved
        }
    return blocks[0]


def pick_bit(values, bit):
    return lax.dynamic_index_in_dim(values, bit, 1, keepdims=False)


def reduce_axis(values, axis):
    place = lax.axis_index(axis)
    for step, mask in enumerate(bits_of(axis)):
        bit = (place >> step) & 1
        halves = values.reshape((values.shape[0] // 2, 2) + values.shape[1:])
        moved = swap(low(pick_bit(halves, 1 - bit)), axis, mask)
        values = pick_bit(halves, bit).astype(jnp.float32) + moved.astype(jnp.float32)
    return values[0]


def small_exp():
    return lax.axis_size("exp") <= 8


def exchange(rows):
    size = lax.axis_size("exp")
    if not small_exp():
        return lax.all_to_all(rows, "exp", split_axis=0, concat_axis=0, tiled=True)
    per = rows.shape[0] // size
    chunks = [rows[index * per : (index + 1) * per] for index in range(size)]
    moved = [chunks[0]] + [swap(chunks[index], "exp", index) for index in range(1, size)]
    return jnp.concatenate(moved, axis=0)


def gather_items(own):
    size = lax.axis_size("exp")
    width = lax.axis_size("hid")
    if not small_exp():
        return lax.all_gather(own, ("exp", "hid"), axis=0, tiled=True)
    near = jnp.concatenate([own] + [swap(own, "hid", mask) for mask in range(1, width)], axis=0)
    rows = jnp.concatenate([near] + [swap(near, "exp", mask) for mask in range(1, size)], axis=0)
    count = own.shape[0]
    place = lax.axis_index("exp") * width + lax.axis_index("hid")
    target = jnp.arange(size * width * count, dtype=jnp.int32)
    source = (target // count ^ place) * count + target % count
    hot = source[:, None] == target[None, :]
    if own.dtype == jnp.bfloat16:
        return low(mat_prod(low(hot), rows))
    return jnp.sum(jnp.where(hot[:, :, None], rows[None, :, :], 0), axis=1)


def sum_all(partial, columns):
    size = lax.axis_size("exp")
    width = lax.axis_size("hid")
    share = partial.shape[0] // (size * width)
    values = partial.reshape(size, width, share, columns)
    place = lax.axis_index("hid")
    for step, mask in enumerate(bits_of("hid")):
        bit = (place >> step) & 1
        halves = values.reshape(size, values.shape[1] // 2, 2, share, columns)
        kept = lax.dynamic_index_in_dim(halves, bit, 2, keepdims=False)
        sent = lax.dynamic_index_in_dim(halves, 1 - bit, 2, keepdims=False)
        moved = swap(low(sent), "hid", mask)
        values = kept.astype(jnp.float32) + moved.astype(jnp.float32)
    mine = low(reduce_axis(values.reshape(size, share, columns), "exp"))
    for step, mask in enumerate(bits_of("hid")):
        bit = (place >> step) & 1
        other = swap(mine, "hid", mask)
        mine = jnp.where(
            bit == 0,
            jnp.concatenate([mine, other], axis=0),
            jnp.concatenate([other, mine], axis=0),
        )
    return mine.astype(jnp.float32)


def condition_of(timesteps, labels, time_weight, time_bias, class_table):
    freq_emb = low(sinus_table(timesteps, time_weight.shape[0]))
    label_hot = low(
        labels[:, None] == jnp.arange(class_table.shape[0], dtype=jnp.int32)[None, :]
    )
    condition = mat_prod(freq_emb, time_weight) + time_bias + mat_prod(label_hot, class_table)
    return freq_emb, label_hot, condition, low(jax.nn.silu(condition))


def per_device(
    patches,
    cotangent,
    timesteps,
    labels,
    routes,
    slot_index,
    time_weight,
    time_bias,
    class_table,
    ada_weight,
    ada_bias,
    qkv_weight,
    proj_weight,
    router_weight,
    shared_in,
    shared_out,
    expert_in,
    expert_out,
):
    tokens, model_dim = patches.shape
    item_count = timesteps.shape[0]
    experts = lax.axis_size("exp")
    place_exp = lax.axis_index("exp")
    capacity = 9 * tokens // (4 * experts)
    slots_all = experts * capacity
    score_scale = 1.0 / math.sqrt(HDIM)

    blocks_in = gather_hid(expert_in[0])
    blocks_out = gather_hid(expert_out[0])
    numbers = gather_items(jnp.stack([timesteps, labels], axis=1))

    freq_emb, label_hot, condition, silu_cond = condition_of(
        timesteps, labels, time_weight, time_bias, class_table
    )
    modulate = mat_prod(silu_cond, ada_weight) + ada_bias
    shift_one, scale_one, gate_one, shift_two, scale_two, gate_two = [
        modulate[:, None, block_index * model_dim : (block_index + 1) * model_dim]
        for block_index in range(6)
    ]
    grad_result = cotangent.astype(jnp.float32).reshape(item_count, SEQ, model_dim)
    grad_branch = (gate_two * grad_result).reshape(tokens, model_dim)
    grad_branch_low = low(grad_branch)

    first_route, second_route = routes[:, 0:1], routes[:, 1:2]
    kept_first = slot_index[:, 0:1] < capacity
    kept_second = slot_index[:, 1:2] < capacity
    slot_ids = jnp.arange(slots_all, dtype=jnp.int32)[None, :]
    first_chunk, second_chunk = first_route, second_route
    if small_exp():
        first_chunk, second_chunk = first_route ^ place_exp, second_route ^ place_exp
    dispatch_first = low(
        (first_chunk * capacity + slot_index[:, 0:1] == slot_ids) & kept_first
    )
    dispatch_second = low(
        (second_chunk * capacity + slot_index[:, 1:2] == slot_ids) & kept_second
    )
    dispatch_both = dispatch_first + dispatch_second
    picks = jnp.concatenate([dispatch_first, dispatch_second], axis=0)
    grad_rows = exchange(low(prod_rows(dispatch_both, grad_branch_low)))
    grad_tokens = jnp.concatenate(gather_hid(grad_branch_low), axis=0)

    residual = patches.astype(jnp.float32).reshape(item_count, SEQ, model_dim)
    normed_one, inverse_one = normalize(residual)
    flat_one = low(normed_one * (1.0 + scale_one) + shift_one).reshape(tokens, model_dim)
    qkv_rows = low(mat_prod(flat_one, qkv_weight)).reshape(item_count, SEQ, 3, HEADS, HDIM)
    queries, key_rows, value_rows = (qkv_rows[:, :, 0], qkv_rows[:, :, 1], qkv_rows[:, :, 2])
    attention = attention_weights(queries, key_rows, score_scale)
    attention_low = low(attention)
    attended = jnp.einsum(
        "bhqk,bkhd->bqhd", attention_low, value_rows, preferred_element_type=jnp.float32
    )
    attended_low = low(attended).reshape(tokens, model_dim)
    branch_one = mat_prod(attended_low, proj_weight).reshape(item_count, SEQ, model_dim)
    residual_one = residual + gate_one * branch_one
    normed_two, inverse_two = normalize(residual_one)
    hidden_two = low(normed_two * (1.0 + scale_two) + shift_two).reshape(tokens, model_dim)
    logits = mat_prod(hidden_two, router_weight)
    expert_ids = jnp.arange(experts, dtype=jnp.int32)[None, :]
    first_hot = (first_route == expert_ids).astype(jnp.float32)
    second_hot = (second_route == expert_ids).astype(jnp.float32)
    logit_gap = jnp.sum(logits * first_hot, axis=1) - jnp.sum(logits * second_hot, axis=1)
    gate_first = jax.nn.sigmoid(logit_gap)[:, None]
    gate_second = 1.0 - gate_first

    lane = jnp.arange(128, dtype=jnp.int32)[None, :]

    def gate_lanes(gate):
        high = low(gate).astype(jnp.float32)
        return low(jnp.where(lane == 0, high, jnp.where(lane == 1, gate - high, 0.0)))

    carried = jnp.concatenate(
        [
            jnp.concatenate([hidden_two, hidden_two], axis=0),
            jnp.concatenate([gate_lanes(gate_first), gate_lanes(gate_second)], axis=0),
        ],
        axis=1,
    )
    received = exchange(low(prod_rows(picks, carried)))
    tokens_all = jnp.concatenate(gather_hid(hidden_two), axis=0)
    rows = received[:, :model_dim]
    gate_rows = (
        received[:, model_dim : model_dim + 1].astype(jnp.float32)
        + received[:, model_dim + 1 : model_dim + 2].astype(jnp.float32)
    )

    pre_shared = mat_prod(tokens_all, shared_in)
    act_shared = low(jax.nn.gelu(pre_shared))
    grad_pre_shared = low(gelu_back(pre_shared, prod_cols(grad_tokens, shared_out)))

    def split(values):
        return [
            values[index * tokens : (index + 1) * tokens] for index in range(lax.axis_size("hid"))
        ]

    shared_term = reduce_hid(split(prod_cols(grad_pre_shared, shared_in)))
    shared_sum = reduce_hid(split(mat_prod(act_shared, shared_out)))

    pre_blocks = [mat_prod(rows, block) for block in blocks_in]
    act_blocks = [low(jax.nn.gelu(block)) for block in pre_blocks]
    expert_rows = low(
        sum(mat_prod(act, block) for act, block in zip(act_blocks, blocks_out))
    )
    back_rows = exchange(expert_rows)
    back_pre = [
        gelu_back(pre, prod_cols(grad_rows, block)) for pre, block in zip(pre_blocks, blocks_out)
    ]
    grad_sent = low(
        sum(prod_cols(low(back), block) for back, block in zip(back_pre, blocks_in))
    )
    grad_back = exchange(grad_sent)
    grad_gated = low(grad_rows.astype(jnp.float32) * gate_rows)
    weight_expert_in = reduce_hid(
        [prod_rows(rows, low(back * gate_rows)) for back in back_pre]
    )
    weight_expert_out = reduce_hid([prod_rows(act, grad_gated) for act in act_blocks])

    weight_shared = jnp.stack(
        [prod_rows(tokens_all, grad_pre_shared), prod_rows(grad_tokens, act_shared)], axis=0
    )
    share = model_dim // experts
    weight_shared = reduce_axis(
        jnp.moveaxis(weight_shared.reshape(2, experts, share, weight_shared.shape[2]), 1, 0), "exp"
    )

    picked = mat_prod(picks, back_rows)
    picked_first, picked_second = picked[:tokens], picked[tokens:]
    moe_out = gate_first * picked_first + gate_second * picked_second
    branch_two = (shared_sum + moe_out).reshape(item_count, SEQ, model_dim)
    output = low(residual_one + gate_two * branch_two).reshape(tokens, model_dim)
    grad_gate_two = jnp.sum(branch_two * grad_result, axis=1)
    grad_gap = (
        jnp.sum(grad_branch * (picked_first - picked_second), axis=1)
        * gate_first[:, 0]
        * gate_second[:, 0]
    )
    grad_logits = low(grad_gap[:, None] * (first_hot - second_hot))
    picked_grad = mat_prod(picks, grad_back)
    grad_hidden = (
        prod_cols(grad_logits, router_weight)
        + shared_term
        + gate_first * picked_grad[:tokens]
        + gate_second * picked_grad[tokens:]
    ).reshape(item_count, SEQ, model_dim)
    grad_shift_two = jnp.sum(grad_hidden, axis=1)
    grad_scale_two = jnp.sum(grad_hidden * normed_two, axis=1)
    grad_residual = grad_result + normalize_back(
        normed_two, inverse_two, grad_hidden * (1.0 + scale_two)
    )
    grad_gate_one = jnp.sum(branch_one * grad_residual, axis=1)
    grad_branch_one = low((gate_one * grad_residual).reshape(tokens, model_dim))
    dense_two = sum_all(
        jnp.concatenate(
            [prod_rows(attended_low, grad_branch_one), prod_rows(hidden_two, grad_logits)], axis=1
        ),
        model_dim + experts,
    )
    counts_local = jnp.sum(
        first_hot * kept_first.astype(jnp.float32) + second_hot * kept_second.astype(jnp.float32),
        axis=0,
    )
    counts_rows = jnp.zeros((item_count, experts), jnp.float32).at[0].set(counts_local)
    early = gather_items(
        low(
            jnp.concatenate(
                [grad_gate_one, grad_shift_two, grad_scale_two, grad_gate_two, counts_rows], axis=1
            )
        )
    )

    grad_attended = low(prod_cols(grad_branch_one, proj_weight)).reshape(
        item_count, SEQ, HEADS, HDIM
    )
    grad_values = jnp.einsum(
        "bhqk,bqhd->bkhd", attention_low, grad_attended, preferred_element_type=jnp.float32
    )
    grad_values = low(grad_values).reshape(tokens, model_dim)
    dense_values = sum_all(prod_rows(flat_one, grad_values), model_dim)
    grad_probs = jnp.einsum(
        "bqhd,bkhd->bhqk", grad_attended, value_rows, preferred_element_type=jnp.float32
    )
    grad_scores = attention * (grad_probs - jnp.sum(attention * grad_probs, axis=-1, keepdims=True))
    grad_scores_low = low(grad_scores * score_scale)
    grad_queries = jnp.einsum(
        "bhqk,bkhd->bqhd", grad_scores_low, key_rows, preferred_element_type=jnp.float32
    )
    grad_keys = jnp.einsum(
        "bhqk,bqhd->bkhd", grad_scores_low, queries, preferred_element_type=jnp.float32
    )
    grad_pair = jnp.concatenate(
        [
            low(grad_queries).reshape(tokens, model_dim),
            low(grad_keys).reshape(tokens, model_dim),
        ],
        axis=1,
    )
    dense_pair = sum_all(prod_rows(flat_one, grad_pair), 2 * model_dim)
    grad_hidden_one = (
        prod_cols(grad_pair, qkv_weight[:, : 2 * model_dim])
        + prod_cols(grad_values, qkv_weight[:, 2 * model_dim :])
    ).reshape(item_count, SEQ, model_dim)
    grad_shift_one = jnp.sum(grad_hidden_one, axis=1)
    grad_scale_one = jnp.sum(grad_hidden_one * normed_one, axis=1)
    grad_input = grad_residual + normalize_back(
        normed_one, inverse_one, grad_hidden_one * (1.0 + scale_one)
    )
    grad_patches = low(grad_input.reshape(tokens, model_dim))
    late = gather_items(low(jnp.concatenate([grad_shift_one, grad_scale_one], axis=1)))

    freq_all, label_all, condition_all, silu_all = condition_of(
        numbers[:, 0], numbers[:, 1], time_weight, time_bias, class_table
    )
    early_mod = early[:, : 4 * model_dim]
    expert_counts = jnp.sum(early[:, 4 * model_dim :].astype(jnp.float32), axis=0)
    silu_share = lax.dynamic_slice_in_dim(silu_all, place_exp * share, share, 1)
    weight_ada = jnp.concatenate(
        [prod_rows(silu_share, late), prod_rows(silu_share, early_mod)], axis=1
    )
    bias_ada = jnp.concatenate(
        [
            jnp.sum(late.astype(jnp.float32), axis=0),
            jnp.sum(early_mod.astype(jnp.float32), axis=0),
        ],
        axis=0,
    )
    grad_silu = prod_cols(early_mod, ada_weight[:, 2 * model_dim :]) + prod_cols(
        late, ada_weight[:, : 2 * model_dim]
    )
    grad_condition = jax.vjp(jax.nn.silu, condition_all)[1](grad_silu)[0]
    bias_time = jnp.sum(grad_condition, axis=0)
    grad_condition_low = low(grad_condition)
    table_grad = prod_rows(label_all, grad_condition_low)
    freq_share = time_weight.shape[0] // experts
    weight_time = prod_rows(
        lax.dynamic_slice_in_dim(freq_all, place_exp * freq_share, freq_share, 1),
        grad_condition_low,
    )
    return (
        output,
        grad_patches,
        weight_time,
        bias_time,
        table_grad,
        weight_ada,
        bias_ada,
        jnp.concatenate([dense_pair, dense_values], axis=1),
        dense_two[:, :model_dim],
        dense_two[:, model_dim:],
        weight_shared[0],
        weight_shared[1].T,
        weight_expert_in[None],
        weight_expert_out[None],
        expert_counts,
    )


def solution(mesh):
    placed = (
        P(("exp", "hid"), None),
        P(("exp", "hid"), None),
        P(("exp", "hid")),
        P(("exp", "hid")),
        P(("exp", "hid"), None),
        P(("exp", "hid"), None),
        P(),
        P(),
        P(),
        P(),
        P(),
        P(),
        P(),
        P(),
        P(None, "hid"),
        P("hid", None),
        P("exp", None, "hid"),
        P("exp", "hid", None),
    )
    return jax.shard_map(
        per_device,
        mesh=mesh,
        in_specs=placed,
        out_specs=(
            P(("exp", "hid"), None),
            P(("exp", "hid"), None),
            P("exp", None),
            P(),
            P(),
            P("exp", None),
            P(),
            P("exp", None),
            P("exp", None),
            P("exp", None),
            P("exp", "hid"),
            P("hid", "exp"),
            P("exp", None, "hid"),
            P("exp", "hid", None),
            P(),
        ),
        check_vma=False,
    )
```

```python
import math

import jax
import jax.numpy as jnp
from jax import lax
from jax.sharding import PartitionSpec as P

HEADS = 12
HDIM = 64
SEQ = 256


eps_norm = 1e-06
highest = lax.Precision.HIGHEST


def mat_prod(left_side, right_side):
    return jnp.dot(left_side, right_side, preferred_element_type=jnp.float32)


def prod_rows(left_side, right_side):
    return lax.dot_general(
        left_side, right_side, (((0,), (0,)), ((), ())), preferred_element_type=jnp.float32
    )


def prod_cols(left_side, right_side):
    return lax.dot_general(
        left_side, right_side, (((1,), (1,)), ((), ())), preferred_element_type=jnp.float32
    )


def sinus_table(timesteps, columns):
    half_cols = columns // 2
    freqs = jnp.exp(-math.log(10000.0) * jnp.arange(half_cols, dtype=jnp.float32) / half_cols)
    angles = timesteps.astype(jnp.float32)[:, None] * freqs[None, :]
    return jnp.concatenate([jnp.cos(angles), jnp.sin(angles)], axis=1)


def normalize(inputs):
    center = inputs - jnp.mean(inputs, axis=-1, keepdims=True)
    inverse = lax.rsqrt(jnp.mean(center * center, axis=-1, keepdims=True) + eps_norm)
    return (center * inverse, inverse)


def normalize_back(normed, inverse, grad_normed):
    return inverse * (
        grad_normed
        - jnp.mean(grad_normed, axis=-1, keepdims=True)
        - normed * jnp.mean(grad_normed * normed, axis=-1, keepdims=True)
    )


def gelu_back(pre_act, grad_act):
    return jax.vjp(jax.nn.gelu, pre_act)[1](grad_act)[0]


def attention_weights(queries, key_rows, score_scale):
    scores = (
        jnp.einsum("bqhd,bkhd->bhqk", queries, key_rows, preferred_element_type=jnp.float32)
        * score_scale
    )
    row_max = jnp.max(scores, axis=-1, keepdims=True)
    log_total = row_max + jnp.log(jnp.sum(jnp.exp(scores - row_max), axis=-1, keepdims=True))
    return jnp.exp(scores - log_total)


def pairs_of(size, mask):
    return [(index, index ^ mask) for index in range(size)]


def swap(values, axis, mask):
    return lax.ppermute(values, axis, pairs_of(lax.axis_size(axis), mask))


def low(values):
    return values.astype(jnp.bfloat16)


def bits_of(axis):
    masks = [1]
    while masks[-1] * 2 < lax.axis_size(axis):
        masks.append(masks[-1] * 2)
    return masks


def gather_hid(own, far):
    masks = bits_of("hid")
    blocks = {0: own, masks[-1]: far}
    for mask in reversed(masks[:-1]):
        for index in list(blocks):
            blocks[index ^ mask] = swap(blocks[index], "hid", mask)
    return [blocks[index] for index in range(lax.axis_size("hid"))]


def gather_rows(own):
    rows = own
    for mask in reversed(bits_of("hid")):
        rows = jnp.concatenate([rows, swap(rows, "hid", mask)], axis=0)
    return rows


def reduce_rows(rows):
    for mask in bits_of("hid"):
        half = rows.shape[0] // 2
        moved = swap(low(rows[half:]), "hid", mask)
        rows = rows[:half].astype(jnp.float32) + moved.astype(jnp.float32)
    return rows


def reduce_hid(blocks):
    blocks = dict(enumerate(blocks))
    for mask in bits_of("hid"):
        moved = {
            index: swap(low(blocks[index | mask]), "hid", mask)
            for index in blocks
            if not index & mask
        }
        blocks = {
            index: blocks[index].astype(jnp.float32) + moved[index].astype(jnp.float32)
            for index in moved
        }
    return blocks[0]


def pick_bit(values, bit):
    return lax.dynamic_index_in_dim(values, bit, 1, keepdims=False)


def reduce_axis(values, axis):
    place = lax.axis_index(axis)
    for step, mask in enumerate(bits_of(axis)):
        bit = (place >> step) & 1
        halves = values.reshape((values.shape[0] // 2, 2) + values.shape[1:])
        moved = swap(low(pick_bit(halves, 1 - bit)), axis, mask)
        values = pick_bit(halves, bit).astype(jnp.float32) + moved.astype(jnp.float32)
    return values[0]


def exchange(rows):
    return lax.all_to_all(rows, "exp", split_axis=0, concat_axis=0, tiled=True)


def join_hid(own):
    place = lax.axis_index("hid")
    for step, mask in reversed(list(enumerate(bits_of("hid")))):
        other = swap(own, "hid", mask)
        both = jnp.stack([own, other], axis=0)
        swapped = jnp.stack([other, own], axis=0)
        own = jnp.where((place >> step) & 1 == 0, both, swapped)
    depth = len(bits_of("hid"))
    own = jnp.transpose(own, tuple(reversed(range(depth))) + tuple(range(depth, own.ndim)))
    return own.reshape((-1,) + own.shape[depth + 1 :])


def gather_items(own):
    near = join_hid(own)
    return exchange(jnp.concatenate([near] * lax.axis_size("exp"), axis=0))


def sum_all(partial):
    size = lax.axis_size("exp")
    width = lax.axis_size("hid")
    columns = partial.shape[1]
    share = partial.shape[0] // (size * width)
    values = partial.reshape(size, width, share, columns)
    place = lax.axis_index("hid")
    for step, mask in enumerate(bits_of("hid")):
        bit = (place >> step) & 1
        halves = values.reshape(size, values.shape[1] // 2, 2, share, columns)
        kept = lax.dynamic_index_in_dim(halves, bit, 2, keepdims=False)
        sent = lax.dynamic_index_in_dim(halves, 1 - bit, 2, keepdims=False)
        moved = swap(low(sent), "hid", mask)
        values = kept.astype(jnp.float32) + moved.astype(jnp.float32)
    parts = exchange(low(values).reshape(size * share, columns)).reshape(size, share, columns)
    mine = low(jnp.sum(parts.astype(jnp.float32), axis=0))
    return join_hid(mine).astype(jnp.float32)


def condition_of(timesteps, labels, time_weight, time_bias, class_table):
    freq_emb = low(sinus_table(timesteps, time_weight.shape[0]))
    label_hot = low(
        labels[:, None] == jnp.arange(class_table.shape[0], dtype=jnp.int32)[None, :]
    )
    condition = mat_prod(freq_emb, time_weight) + time_bias + mat_prod(label_hot, class_table)
    return freq_emb, label_hot, condition, low(jax.nn.silu(condition))


def per_device(
    patches,
    cotangent,
    timesteps,
    labels,
    routes,
    slot_index,
    time_weight,
    time_bias,
    class_table,
    ada_weight,
    ada_bias,
    qkv_weight,
    proj_weight,
    router_weight,
    shared_in,
    shared_out,
    expert_in,
    expert_out,
):
    tokens, model_dim = patches.shape
    item_count = timesteps.shape[0]
    experts = lax.axis_size("exp")
    place_exp = lax.axis_index("exp")
    capacity = 9 * tokens // (4 * experts)
    slots_all = experts * capacity
    score_scale = 1.0 / math.sqrt(HDIM)

    own_in, own_out = expert_in[0], expert_out[0]
    far_mask = bits_of("hid")[-1]
    far_in = swap(own_in, "hid", far_mask)
    far_in, later_out = lax.optimization_barrier((far_in, own_out))
    far_out = swap(later_out, "hid", far_mask)

    freq_emb, label_hot, condition, silu_cond = condition_of(
        timesteps, labels, time_weight, time_bias, class_table
    )
    modulate = mat_prod(silu_cond, ada_weight) + ada_bias
    shift_one, scale_one, gate_one, shift_two, scale_two, gate_two = [
        modulate[:, None, block_index * model_dim : (block_index + 1) * model_dim]
        for block_index in range(6)
    ]
    grad_result = cotangent.astype(jnp.float32).reshape(item_count, SEQ, model_dim)
    grad_branch = (gate_two * grad_result).reshape(tokens, model_dim)
    grad_branch_low = low(grad_branch)

    first_route, second_route = routes[:, 0:1], routes[:, 1:2]
    kept_first = slot_index[:, 0:1] < capacity
    kept_second = slot_index[:, 1:2] < capacity
    slot_ids = jnp.arange(slots_all, dtype=jnp.int32)[None, :]
    dispatch_first = low(
        (first_route * capacity + slot_index[:, 0:1] == slot_ids) & kept_first
    )
    dispatch_second = low(
        (second_route * capacity + slot_index[:, 1:2] == slot_ids) & kept_second
    )
    dispatch_both = dispatch_first + dispatch_second
    picks = jnp.concatenate([dispatch_first, dispatch_second], axis=0)
    grad_rows = exchange(low(prod_rows(dispatch_both, grad_branch_low)))
    grad_tokens = gather_rows(grad_branch_low)

    residual = patches.astype(jnp.float32).reshape(item_count, SEQ, model_dim)
    normed_one, inverse_one = normalize(residual)
    flat_one = low(normed_one * (1.0 + scale_one) + shift_one).reshape(tokens, model_dim)
    qkv_rows = low(mat_prod(flat_one, qkv_weight)).reshape(item_count, SEQ, 3, HEADS, HDIM)
    queries, key_rows, value_rows = (qkv_rows[:, :, 0], qkv_rows[:, :, 1], qkv_rows[:, :, 2])
    attention = attention_weights(queries, key_rows, score_scale)
    attention_low = low(attention)
    attended = jnp.einsum(
        "bhqk,bkhd->bqhd", attention_low, value_rows, preferred_element_type=jnp.float32
    )
    attended_low = low(attended).reshape(tokens, model_dim)
    branch_one = mat_prod(attended_low, proj_weight).reshape(item_count, SEQ, model_dim)
    residual_one = residual + gate_one * branch_one
    normed_two, inverse_two = normalize(residual_one)
    hidden_two = low(normed_two * (1.0 + scale_two) + shift_two).reshape(tokens, model_dim)
    logits = mat_prod(hidden_two, router_weight)
    expert_ids = jnp.arange(experts, dtype=jnp.int32)[None, :]
    first_hot = (first_route == expert_ids).astype(jnp.float32)
    second_hot = (second_route == expert_ids).astype(jnp.float32)
    logit_gap = jnp.sum(logits * first_hot, axis=1) - jnp.sum(logits * second_hot, axis=1)
    gate_first = jax.nn.sigmoid(logit_gap)[:, None]
    gate_second = 1.0 - gate_first

    lane = jnp.arange(128, dtype=jnp.int32)[None, :]

    def gate_lanes(gate):
        high = low(gate).astype(jnp.float32)
        return low(jnp.where(lane == 0, high, jnp.where(lane == 1, gate - high, 0.0)))

    carried = jnp.concatenate(
        [
            jnp.concatenate([hidden_two, hidden_two], axis=0),
            jnp.concatenate([gate_lanes(gate_first), gate_lanes(gate_second)], axis=0),
        ],
        axis=1,
    )
    sent_rows, grad_rows, far_in = lax.optimization_barrier(
        (low(prod_rows(picks, carried)), grad_rows, far_in)
    )
    received = exchange(sent_rows)
    blocks_in = gather_hid(own_in, far_in)
    blocks_out = gather_hid(own_out, far_out)
    tokens_all = gather_rows(hidden_two)
    rows = received[:, :model_dim]
    gate_rows = (
        received[:, model_dim : model_dim + 1].astype(jnp.float32)
        + received[:, model_dim + 1 : model_dim + 2].astype(jnp.float32)
    )

    pre_shared = mat_prod(tokens_all, shared_in)
    act_shared = low(jax.nn.gelu(pre_shared))
    grad_pre_shared = low(gelu_back(pre_shared, prod_cols(grad_tokens, shared_out)))

    shared_term = reduce_rows(prod_cols(grad_pre_shared, shared_in))
    shared_sum = reduce_rows(mat_prod(act_shared, shared_out))

    pre_blocks = [mat_prod(rows, block) for block in blocks_in]
    act_blocks = [low(jax.nn.gelu(block)) for block in pre_blocks]
    expert_rows = low(
        sum(mat_prod(act, block) for act, block in zip(act_blocks, blocks_out))
    )
    back_rows = exchange(expert_rows)
    back_pre = [
        gelu_back(pre, prod_cols(grad_rows, block)) for pre, block in zip(pre_blocks, blocks_out)
    ]
    grad_sent = low(
        sum(prod_cols(low(back), block) for back, block in zip(back_pre, blocks_in))
    )
    grad_back = exchange(grad_sent)
    grad_gated = low(grad_rows.astype(jnp.float32) * gate_rows)
    weight_expert_in = reduce_hid(
        [prod_rows(rows, low(back * gate_rows)) for back in back_pre]
    )
    weight_expert_out = reduce_hid([prod_rows(act, grad_gated) for act in act_blocks])

    weight_shared = jnp.stack(
        [prod_rows(tokens_all, grad_pre_shared), prod_rows(grad_tokens, act_shared)], axis=0
    )
    share = model_dim // experts
    weight_shared = reduce_axis(
        jnp.moveaxis(weight_shared.reshape(2, experts, share, weight_shared.shape[2]), 1, 0), "exp"
    )

    picked = mat_prod(picks, back_rows)
    picked_first, picked_second = picked[:tokens], picked[tokens:]
    moe_out = gate_first * picked_first + gate_second * picked_second
    branch_two = (shared_sum + moe_out).reshape(item_count, SEQ, model_dim)
    output = low(residual_one + gate_two * branch_two).reshape(tokens, model_dim)
    grad_gate_two = jnp.sum(branch_two * grad_result, axis=1)
    grad_gap = (
        jnp.sum(grad_branch * (picked_first - picked_second), axis=1)
        * gate_first[:, 0]
        * gate_second[:, 0]
    )
    grad_logits = low(grad_gap[:, None] * (first_hot - second_hot))
    picked_grad = mat_prod(picks, grad_back)
    grad_hidden = (
        prod_cols(grad_logits, router_weight)
        + shared_term
        + gate_first * picked_grad[:tokens]
        + gate_second * picked_grad[tokens:]
    ).reshape(item_count, SEQ, model_dim)
    grad_shift_two = jnp.sum(grad_hidden, axis=1)
    grad_scale_two = jnp.sum(grad_hidden * normed_two, axis=1)
    grad_residual = grad_result + normalize_back(
        normed_two, inverse_two, grad_hidden * (1.0 + scale_two)
    )
    grad_gate_one = jnp.sum(branch_one * grad_residual, axis=1)
    grad_branch_one = low((gate_one * grad_residual).reshape(tokens, model_dim))
    grad_attended = low(prod_cols(grad_branch_one, proj_weight)).reshape(
        item_count, SEQ, HEADS, HDIM
    )
    grad_values = jnp.einsum(
        "bhqk,bqhd->bkhd", attention_low, grad_attended, preferred_element_type=jnp.float32
    )
    grad_values = low(grad_values).reshape(tokens, model_dim)
    padded = jnp.pad(grad_logits, ((0, 0), (0, -experts % 128)))
    dense_one = sum_all(
        jnp.concatenate(
            [
                low(prod_rows(attended_low, grad_branch_one)),
                low(prod_rows(flat_one, grad_values)),
                low(prod_rows(hidden_two, padded)),
            ],
            axis=1,
        )
    )
    grad_probs = jnp.einsum(
        "bqhd,bkhd->bhqk", grad_attended, value_rows, preferred_element_type=jnp.float32
    )
    grad_scores = attention * (grad_probs - jnp.sum(attention * grad_probs, axis=-1, keepdims=True))
    grad_scores_low = low(grad_scores * score_scale)
    grad_queries = jnp.einsum(
        "bhqk,bkhd->bqhd", grad_scores_low, key_rows, preferred_element_type=jnp.float32
    )
    grad_keys = jnp.einsum(
        "bhqk,bqhd->bkhd", grad_scores_low, queries, preferred_element_type=jnp.float32
    )
    grad_pair = jnp.concatenate(
        [
            low(grad_queries).reshape(tokens, model_dim),
            low(grad_keys).reshape(tokens, model_dim),
        ],
        axis=1,
    )
    pair_rows, weight_expert_in, weight_expert_out, weight_shared = lax.optimization_barrier(
        (grad_pair, weight_expert_in, weight_expert_out, weight_shared)
    )
    dense_pair = sum_all(prod_rows(flat_one, pair_rows))
    grad_hidden_one = (
        prod_cols(grad_pair, qkv_weight[:, : 2 * model_dim])
        + prod_cols(grad_values, qkv_weight[:, 2 * model_dim :])
    ).reshape(item_count, SEQ, model_dim)
    grad_shift_one = jnp.sum(grad_hidden_one, axis=1)
    grad_scale_one = jnp.sum(grad_hidden_one * normed_one, axis=1)
    grad_input = grad_residual + normalize_back(
        normed_one, inverse_one, grad_hidden_one * (1.0 + scale_one)
    )
    grad_patches = low(grad_input.reshape(tokens, model_dim))
    counts_local = jnp.sum(
        first_hot * kept_first.astype(jnp.float32) + second_hot * kept_second.astype(jnp.float32),
        axis=0,
    )
    counts_rows = jnp.where(jnp.arange(item_count)[:, None] == 0, counts_local[None, :], 0.0)
    digits = jnp.stack(
        [timesteps // 32, timesteps % 32, labels // 32, labels % 32], axis=1
    ).astype(jnp.float32)
    item_rows = gather_items(
        low(
            jnp.concatenate(
                [
                    grad_shift_one,
                    grad_scale_one,
                    grad_gate_one,
                    grad_shift_two,
                    grad_scale_two,
                    grad_gate_two,
                    digits,
                    counts_rows,
                ],
                axis=1,
            )
        )
    )

    grad_modulate = item_rows[:, : 6 * model_dim]
    rest = item_rows[:, 6 * model_dim :].astype(jnp.float32)
    expert_counts = jnp.sum(rest[:, 4:], axis=0)
    numbers = rest[:, 0:4:2] * 32.0 + rest[:, 1:4:2]
    freq_all, label_all, condition_all, silu_all = condition_of(
        numbers[:, 0].astype(jnp.int32),
        numbers[:, 1].astype(jnp.int32),
        time_weight,
        time_bias,
        class_table,
    )
    weight_ada = prod_rows(
        lax.dynamic_slice_in_dim(silu_all, place_exp * share, share, 1), grad_modulate
    )
    bias_ada = jnp.sum(grad_modulate.astype(jnp.float32), axis=0)
    grad_silu = prod_cols(grad_modulate, ada_weight)
    grad_condition = jax.vjp(jax.nn.silu, condition_all)[1](grad_silu)[0]
    bias_time = jnp.sum(grad_condition, axis=0)
    grad_condition_low = low(grad_condition)
    table_grad = prod_rows(label_all, grad_condition_low)
    freq_share = time_weight.shape[0] // experts
    weight_time = prod_rows(
        lax.dynamic_slice_in_dim(freq_all, place_exp * freq_share, freq_share, 1),
        grad_condition_low,
    )
    return (
        output,
        grad_patches,
        weight_time,
        bias_time,
        table_grad,
        weight_ada,
        bias_ada,
        jnp.concatenate([dense_pair, dense_one[:, model_dim : 2 * model_dim]], axis=1),
        dense_one[:, :model_dim],
        dense_one[:, 2 * model_dim : 2 * model_dim + experts],
        weight_shared[0],
        weight_shared[1].T,
        weight_expert_in[None],
        weight_expert_out[None],
        expert_counts,
    )


def solution(mesh):
    placed = (
        P(("exp", "hid"), None),
        P(("exp", "hid"), None),
        P(("exp", "hid")),
        P(("exp", "hid")),
        P(("exp", "hid"), None),
        P(("exp", "hid"), None),
        P(),
        P(),
        P(),
        P(),
        P(),
        P(),
        P(),
        P(),
        P(None, "hid"),
        P("hid", None),
        P("exp", None, "hid"),
        P("exp", "hid", None),
    )
    return jax.shard_map(
        per_device,
        mesh=mesh,
        in_specs=placed,
        out_specs=(
            P(("exp", "hid"), None),
            P(("exp", "hid"), None),
            P("exp", None),
            P(),
            P(),
            P("exp", None),
            P(),
            P("exp", None),
            P("exp", None),
            P("exp", None),
            P("exp", "hid"),
            P("hid", "exp"),
            P("exp", None, "hid"),
            P("exp", "hid", None),
            P(),
        ),
        check_vma=False,
    )
```

```python
import functools
import math

import jax
import jax.numpy as jnp
from jax import lax
from jax.experimental import pallas as pl
from jax.experimental.pallas import tpu as pltpu
from jax.sharding import PartitionSpec as P

HEADS = 12
HDIM = 64
SEQ = 256


eps_norm = 1e-06
highest = lax.Precision.HIGHEST


def mat_prod(left_side, right_side):
    return jnp.dot(left_side, right_side, preferred_element_type=jnp.float32)


def prod_rows(left_side, right_side):
    return lax.dot_general(
        left_side, right_side, (((0,), (0,)), ((), ())), preferred_element_type=jnp.float32
    )


def prod_cols(left_side, right_side):
    return lax.dot_general(
        left_side, right_side, (((1,), (1,)), ((), ())), preferred_element_type=jnp.float32
    )


def sinus_table(timesteps, columns):
    half_cols = columns // 2
    freqs = jnp.exp(-math.log(10000.0) * jnp.arange(half_cols, dtype=jnp.float32) / half_cols)
    angles = timesteps.astype(jnp.float32)[:, None] * freqs[None, :]
    return jnp.concatenate([jnp.cos(angles), jnp.sin(angles)], axis=1)


def normalize(inputs):
    center = inputs - jnp.mean(inputs, axis=-1, keepdims=True)
    inverse = lax.rsqrt(jnp.mean(center * center, axis=-1, keepdims=True) + eps_norm)
    return (center * inverse, inverse)


def normalize_back(normed, inverse, grad_normed):
    return inverse * (
        grad_normed
        - jnp.mean(grad_normed, axis=-1, keepdims=True)
        - normed * jnp.mean(grad_normed * normed, axis=-1, keepdims=True)
    )


def pairs_of(size, mask):
    return [(index, index ^ mask) for index in range(size)]


def swap(values, axis, mask):
    return lax.ppermute(values, axis, pairs_of(lax.axis_size(axis), mask))


def low(values):
    return values.astype(jnp.bfloat16)


def bits_of(axis):
    masks = [1]
    while masks[-1] * 2 < lax.axis_size(axis):
        masks.append(masks[-1] * 2)
    return masks


def gather_hid(own, far):
    masks = bits_of("hid")
    blocks = {0: own, masks[-1]: far}
    for mask in reversed(masks[:-1]):
        for index in list(blocks):
            blocks[index ^ mask] = swap(blocks[index], "hid", mask)
    return [blocks[index] for index in range(lax.axis_size("hid"))]


def gather_rows(own):
    masks = bits_of("hid")
    rows, first = own, own
    for mask in reversed(masks[1:]):
        moved = swap(rows, "hid", mask)
        first = moved if rows is own else first
        rows = jnp.concatenate([rows, moved], axis=0)
    return (rows, swap(rows, "hid", masks[0])), first


def after(values, other):
    seen = other.reshape(-1)[0].astype(jnp.float32)
    return jnp.where(seen == seen, values, jnp.zeros_like(values))


def reduce_rows(halves):
    first = swap(halves[1], "hid", bits_of("hid")[0])
    return halves[0].astype(jnp.float32) + first.astype(jnp.float32), first


def reduce_more(rows):
    for mask in bits_of("hid")[1:]:
        half = rows.shape[0] // 2
        moved = swap(low(rows[half:]), "hid", mask)
        rows = rows[:half] + moved.astype(jnp.float32)
    return rows


def reduce_step(values, axis, step):
    bit = (lax.axis_index(axis) >> step) & 1
    halves = values.reshape((values.shape[0], values.shape[1] // 2, 2) + values.shape[2:])
    kept = lax.dynamic_index_in_dim(halves, bit, 2, keepdims=False)
    sent = lax.dynamic_index_in_dim(halves, 1 - bit, 2, keepdims=False)
    return kept.astype(jnp.float32) + swap(low(sent), axis, 1 << step).astype(jnp.float32)


def spread_rest(values):
    left = values.shape[1]
    if left > 4:
        for step in range(1, len(bits_of("exp"))):
            values = reduce_step(values, "exp", step)
        return [values[:, 0]]
    place = lax.axis_index("exp") >> 1
    parts = [lax.dynamic_index_in_dim(values, place ^ mask, 1, keepdims=False) for mask in range(left)]
    return parts[:1] + [swap(low(parts[mask]), "exp", 2 * mask) for mask in range(1, left)]


def exchange(rows):
    return lax.all_to_all(rows, "exp", split_axis=0, concat_axis=0, tiled=True)


def join_hid(own):
    place = lax.axis_index("hid")
    for step, mask in reversed(list(enumerate(bits_of("hid")))):
        other = swap(own, "hid", mask)
        both = jnp.stack([own, other], axis=0)
        swapped = jnp.stack([other, own], axis=0)
        own = jnp.where((place >> step) & 1 == 0, both, swapped)
    depth = len(bits_of("hid"))
    own = jnp.transpose(own, tuple(reversed(range(depth))) + tuple(range(depth, own.ndim)))
    return own.reshape((-1,) + own.shape[depth + 1 :])


def gather_items(own, gate):
    count = own.shape[0]
    width = lax.axis_size("hid")
    rows, offsets = own, [0]
    for axis, weight in (("exp", width), ("hid", 1)):
        for mask in bits_of(axis):
            rows = jnp.concatenate([rows, swap(rows, axis, mask)], axis=0)
            offsets = offsets + [offset ^ (mask * weight) for offset in offsets]
        if axis == "exp":
            rows, gate = lax.optimization_barrier((rows, gate))
    place = lax.axis_index("exp") * width + lax.axis_index("hid")
    part = jnp.arange(len(offsets) * count, dtype=jnp.int32)
    source = (jnp.repeat(jnp.array(offsets, jnp.int32), count) ^ place) * count + part % count
    return low(mat_prod(low(source[None, :] == part[:, None]), rows)), gate


def sum_hid(partial, gates):
    size = lax.axis_size("exp")
    width = lax.axis_size("hid")
    columns = partial.shape[1]
    share = partial.shape[0] // (size * width)
    values = partial.reshape(size, width, share, columns)
    place = lax.axis_index("hid")
    masks = bits_of("hid")
    for step, mask in enumerate(masks):
        bit = (place >> step) & 1
        halves = values.reshape(size, values.shape[1] // 2, 2, share, columns)
        kept = lax.dynamic_index_in_dim(halves, bit, 2, keepdims=False)
        sent = low(lax.dynamic_index_in_dim(halves, 1 - bit, 2, keepdims=False))
        if mask == masks[-1]:
            sent, gates = lax.optimization_barrier((sent, gates))
        values = kept.astype(jnp.float32) + swap(sent, "hid", mask).astype(jnp.float32)
    return low(values).reshape(size * share, columns), gates


def sum_parts(values):
    size = lax.axis_size("exp")
    parts = values.reshape(size, values.shape[0] // size, values.shape[1])
    return join_hid(low(jnp.sum(parts.astype(jnp.float32), axis=0))).astype(jnp.float32)


SMALL_COST = pl.CostEstimate(flops=1000, bytes_accessed=1000, transcendentals=0)


def gelu_pair(pre):
    square = pre * pre
    scale = math.sqrt(2.0 / math.pi)
    bent = jnp.tanh(pre * (scale + (scale * 0.044715) * square))
    half = 0.5 + 0.5 * bent
    slope = half + (0.5 * pre) * (1.0 - bent * bent) * (scale + (3.0 * scale * 0.044715) * square)
    return pre * half, slope


def expert_body(block_count, width, gated, *refs):
    rows_ref, grads_ref = refs[0], refs[1]
    in_refs = refs[2 : 2 + block_count]
    out_refs = refs[2 + block_count : 2 + 2 * block_count]
    rest = refs[2 + 2 * block_count :]
    if gated:
        back_ref, sum_ref, scaled_ref = rest[:3]
        rest = rest[3:]
    else:
        back_ref, sum_ref = rest[:2]
        rest = rest[2:]
    act_refs, slope_refs = rest[:block_count], rest[block_count : 2 * block_count]
    pre_ref, hidden_ref, low_ref, sum_acc, back_acc = rest[2 * block_count :]
    count = rows_ref.shape[0]
    step = 32
    for index in range(block_count):
        pre_ref[...] = mat_prod(rows_ref[:, :width], in_refs[index][...])
        hidden_ref[...] = prod_cols(grads_ref[...], out_refs[index][...])

        def bend(place, carry, index=index):
            span = pl.ds(pl.multiple_of(place * step, step), step)
            act, slope = gelu_pair(pre_ref[span, :])
            back = hidden_ref[span, :] * slope
            act_refs[index][span, :] = low(act)
            if gated:
                low_ref[span, :] = low(back)
                gate = rows_ref[span, width : width + 128].astype(jnp.float32)
                slope_refs[index][span, :] = low(back * (gate[:, 0:1] + gate[:, 1:2]))
            else:
                slope_refs[index][span, :] = low(back)
            return carry

        lax.fori_loop(0, count // step, bend, 0)
        part_sum = mat_prod(act_refs[index][...], out_refs[index][...])
        sent = low_ref if gated else slope_refs[index]
        part_back = prod_cols(sent[...], in_refs[index][...])
        if index == 0:
            sum_acc[...] = part_sum
            back_acc[...] = part_back
        else:
            sum_acc[...] += part_sum
            back_acc[...] += part_back

    def finish(place, carry):
        span = pl.ds(pl.multiple_of(place * step, step), step)
        total = sum_acc[span, :]
        sum_ref[span, :] = low(total)
        back_ref[span, :width] = low(back_acc[span, :])
        if gated:
            grads = grads_ref[span, :].astype(jnp.float32)
            gate = rows_ref[span, width : width + 128].astype(jnp.float32)
            scaled_ref[span, :] = low(grads * (gate[:, 0:1] + gate[:, 1:2]))
            dots = jnp.sum(total * grads, axis=1, keepdims=True)
            high = low(dots).astype(jnp.float32)
            lane = lax.broadcasted_iota(jnp.int32, (step, 128), 1)
            back_ref[span, width : width + 128] = low(
                jnp.where(lane == 0, high, jnp.where(lane == 1, dots - high, 0.0))
            )
        return carry

    lax.fori_loop(0, count // step, finish, 0)


def expert_pass(rows, grads, blocks_in, blocks_out, gated):
    count, width = grads.shape
    hidden = blocks_in[0].shape[1]
    blocks = len(blocks_in)

    def shape(columns):
        return jax.ShapeDtypeStruct((count, columns), jnp.bfloat16)

    outs = [shape(rows.shape[1]), shape(width)] + ([shape(width)] if gated else [])
    outs += [shape(hidden)] * (2 * blocks)
    scratch = [
        pltpu.VMEM((count, hidden), jnp.float32),
        pltpu.VMEM((count, hidden), jnp.float32),
        pltpu.VMEM((count, hidden), jnp.bfloat16),
        pltpu.VMEM((count, width), jnp.float32),
        pltpu.VMEM((count, width), jnp.float32),
    ]
    return pl.pallas_call(
        functools.partial(expert_body, blocks, width, gated),
        out_shape=outs,
        scratch_shapes=scratch,
        cost_estimate=SMALL_COST,
        compiler_params=pltpu.CompilerParams(vmem_limit_bytes=56 * 1024 * 1024),
    )(rows, grads, *blocks_in, *blocks_out)


def outer_body(block_count, width, added, *refs):
    rows_ref, grads_ref = refs[0], refs[1]
    parts = [
        refs[2 + kind * block_count : 2 + (kind + 1) * block_count] for kind in range(6 if added else 4)
    ]
    act_refs, back_refs = parts[:2]
    in_refs, out_refs = parts[-2:]
    for index in range(block_count):
        first = prod_rows(rows_ref[:, :width], back_refs[index][...])
        second = prod_rows(act_refs[index][...], grads_ref[...])
        if added:
            first += parts[2][index][...].astype(jnp.float32)
            second += parts[3][index][...].astype(jnp.float32)
        in_refs[index][...] = low(first)
        out_refs[index][...] = low(second)


def outer_pass(rows, grads, acts, backs, added=()):
    width, hidden, blocks = grads.shape[1], acts[0].shape[1], len(acts)
    outs = [jax.ShapeDtypeStruct((width, hidden), jnp.bfloat16)] * blocks
    outs += [jax.ShapeDtypeStruct((hidden, width), jnp.bfloat16)] * blocks
    made = pl.pallas_call(
        functools.partial(outer_body, blocks, width, bool(added)),
        out_shape=outs,
        cost_estimate=SMALL_COST,
        compiler_params=pltpu.CompilerParams(vmem_limit_bytes=56 * 1024 * 1024),
    )(rows, grads, *acts, *backs, *added)
    return made[:blocks], made[blocks:]


def shared_body(rows_a, rows_b, grads_a, grads_b, act_a, act_b, back_a, back_b, out_ref):
    out_ref[0] = low(prod_rows(rows_a[...], back_a[...]) + prod_rows(rows_b[...], back_b[...]))
    out_ref[1] = low(prod_rows(grads_a[...], act_a[...]) + prod_rows(grads_b[...], act_b[...]))


def shared_outer(*arrays):
    return pl.pallas_call(
        shared_body,
        out_shape=jax.ShapeDtypeStruct((2, arrays[0].shape[1], arrays[4].shape[1]), jnp.bfloat16),
        cost_estimate=SMALL_COST,
        compiler_params=pltpu.CompilerParams(vmem_limit_bytes=56 * 1024 * 1024),
    )(*arrays)


def head_weights(queries, key_rows, score_scale):
    scores = prod_cols(queries, key_rows) * score_scale
    raised = jnp.exp(scores - jnp.max(scores, axis=1, keepdims=True))
    return raised / jnp.sum(raised, axis=1, keepdims=True)


def pair_spans(pair, width):
    return [pl.ds(pl.multiple_of(part * width + pair * 128, 128), 128) for part in range(3)]


def attend_body(score_scale, rows_ref, out_ref):
    width = out_ref.shape[1]
    lane = lax.broadcasted_iota(jnp.int32, (out_ref.shape[0], 128), 1)

    def step(pair, carry):
        at_q, at_k, at_v = pair_spans(pair, width)
        queries, keys, values = rows_ref[:, at_q], rows_ref[:, at_k], rows_ref[:, at_v]
        sides = []
        for side in range(2):
            mine = (lane >= side * HDIM) & (lane < (side + 1) * HDIM)
            weights = head_weights(jnp.where(mine, queries, 0), keys, score_scale)
            sides.append(mat_prod(low(weights), values))
        out_ref[:, at_q] = low(jnp.where(lane < HDIM, sides[0], sides[1]))
        return carry

    lax.fori_loop(0, width // 128, step, 0)


def attend_back_body(score_scale, rows_ref, grad_ref, out_ref):
    width = grad_ref.shape[1]
    lane = lax.broadcasted_iota(jnp.int32, (grad_ref.shape[0], 128), 1)

    def step(pair, carry):
        at_q, at_k, at_v = pair_spans(pair, width)
        queries, keys, values = rows_ref[:, at_q], rows_ref[:, at_k], rows_ref[:, at_v]
        grads = grad_ref[:, at_q]
        to_q, to_k, to_v = [], [], []
        for side in range(2):
            mine = (lane >= side * HDIM) & (lane < (side + 1) * HDIM)
            head_queries, head_grads = jnp.where(mine, queries, 0), jnp.where(mine, grads, 0)
            weights = head_weights(head_queries, keys, score_scale)
            to_v.append(prod_rows(low(weights), head_grads))
            probs = prod_cols(head_grads, values)
            inner = jnp.sum(weights * probs, axis=1, keepdims=True)
            scores = low(weights * (probs - inner) * score_scale)
            to_q.append(mat_prod(scores, keys))
            to_k.append(prod_rows(scores, head_queries))
        out_ref[:, at_q] = low(jnp.where(lane < HDIM, to_q[0], to_q[1]))
        out_ref[:, at_k] = low(to_k[0] + to_k[1])
        out_ref[:, at_v] = low(to_v[0] + to_v[1])
        return carry

    lax.fori_loop(0, width // 128, step, 0)


def attend(body, arrays, columns, score_scale):
    rows = arrays[0].shape[0]
    return pl.pallas_call(
        functools.partial(body, score_scale),
        grid=(rows // SEQ,),
        in_specs=[pl.BlockSpec((SEQ, array.shape[1]), lambda item: (item, 0)) for array in arrays],
        out_specs=pl.BlockSpec((SEQ, columns), lambda item: (item, 0)),
        out_shape=jax.ShapeDtypeStruct((rows, columns), jnp.bfloat16),
        cost_estimate=SMALL_COST,
    )(*arrays)


def condition_of(timesteps, labels, time_weight, time_bias, class_table):
    freq_emb = low(sinus_table(timesteps, time_weight.shape[0]))
    label_hot = low(
        labels[:, None] == jnp.arange(class_table.shape[0], dtype=jnp.int32)[None, :]
    )
    condition = mat_prod(freq_emb, time_weight) + time_bias + mat_prod(label_hot, class_table)
    return freq_emb, label_hot, condition, low(jax.nn.silu(condition))


def per_device(
    patches,
    cotangent,
    timesteps,
    labels,
    routes,
    slot_index,
    time_weight,
    time_bias,
    class_table,
    ada_weight,
    ada_bias,
    qkv_weight,
    proj_weight,
    router_weight,
    shared_in,
    shared_out,
    expert_in,
    expert_out,
):
    tokens, model_dim = patches.shape
    item_count = timesteps.shape[0]
    experts = lax.axis_size("exp")
    place_exp = lax.axis_index("exp")
    capacity = 9 * tokens // (4 * experts)
    slots_all = experts * capacity
    score_scale = 1.0 / math.sqrt(HDIM)

    own_in, own_out = expert_in[0], expert_out[0]
    far_mask = bits_of("hid")[-1]
    far_in = swap(own_in, "hid", far_mask)

    freq_emb, label_hot, condition, silu_cond = condition_of(
        timesteps, labels, time_weight, time_bias, class_table
    )
    modulate = mat_prod(silu_cond, ada_weight) + ada_bias
    shift_one, scale_one, gate_one, shift_two, scale_two, gate_two = [
        modulate[:, None, block_index * model_dim : (block_index + 1) * model_dim]
        for block_index in range(6)
    ]
    grad_result = cotangent.astype(jnp.float32).reshape(item_count, SEQ, model_dim)
    grad_branch = (gate_two * grad_result).reshape(tokens, model_dim)
    grad_branch_low = low(grad_branch)

    first_route, second_route = routes[:, 0:1], routes[:, 1:2]
    kept_first = slot_index[:, 0:1] < capacity
    kept_second = slot_index[:, 1:2] < capacity
    slot_ids = jnp.arange(slots_all, dtype=jnp.int32)[None, :]
    dispatch_first = low(
        (first_route * capacity + slot_index[:, 0:1] == slot_ids) & kept_first
    )
    dispatch_second = low(
        (second_route * capacity + slot_index[:, 1:2] == slot_ids) & kept_second
    )
    dispatch_both = dispatch_first + dispatch_second
    picks = jnp.concatenate([dispatch_first, dispatch_second], axis=0)
    grad_rows = exchange(low(prod_rows(dispatch_both, grad_branch_low)))
    grad_tokens, _ = gather_rows(grad_branch_low)

    residual = patches.astype(jnp.float32).reshape(item_count, SEQ, model_dim)
    normed_one, inverse_one = normalize(residual)
    flat_one = low(normed_one * (1.0 + scale_one) + shift_one).reshape(tokens, model_dim)
    qkv_rows = low(mat_prod(flat_one, qkv_weight))
    qkv_rows, far_in = lax.optimization_barrier((qkv_rows, far_in))
    attended_low = attend(attend_body, [qkv_rows], model_dim, score_scale)
    branch_one = mat_prod(attended_low, proj_weight).reshape(item_count, SEQ, model_dim)
    residual_one = residual + gate_one * branch_one
    normed_two, inverse_two = normalize(residual_one)
    hidden_two = low(normed_two * (1.0 + scale_two) + shift_two).reshape(tokens, model_dim)
    logits = mat_prod(hidden_two, router_weight)
    expert_ids = jnp.arange(experts, dtype=jnp.int32)[None, :]
    first_hot = (first_route == expert_ids).astype(jnp.float32)
    second_hot = (second_route == expert_ids).astype(jnp.float32)
    logit_gap = jnp.sum(logits * first_hot, axis=1) - jnp.sum(logits * second_hot, axis=1)
    gate_first = jax.nn.sigmoid(logit_gap)[:, None]
    gate_second = 1.0 - gate_first

    lane = jnp.arange(128, dtype=jnp.int32)[None, :]

    def gate_lanes(gate):
        high = low(gate).astype(jnp.float32)
        return low(jnp.where(lane == 0, high, jnp.where(lane == 1, gate - high, 0.0)))

    carried = jnp.concatenate(
        [
            jnp.concatenate([hidden_two, hidden_two], axis=0),
            jnp.concatenate([gate_lanes(gate_first), gate_lanes(gate_second)], axis=0),
        ],
        axis=1,
    )
    sent_rows, grad_rows = lax.optimization_barrier((low(prod_rows(picks, carried)), grad_rows))
    received = exchange(sent_rows)
    blocks_in = gather_hid(own_in, far_in)
    tokens_all, first_tokens = gather_rows(hidden_two)
    far_out = swap(after(own_out, first_tokens[:1, :128]), "hid", far_mask)
    blocks_out = gather_hid(own_out, far_out)

    halves = [
        expert_pass(rows, grads, [shared_in], [shared_out], False)
        for rows, grads in zip(tokens_all, grad_tokens)
    ]
    term_part, sum_part, act_shared, back_shared = zip(*halves)
    shared_term = reduce_more(reduce_rows(term_part)[0])
    weight_shared = shared_outer(*tokens_all, *grad_tokens, *act_shared, *back_shared)

    received, weight_shared = lax.optimization_barrier((received, weight_shared))
    share = model_dim // experts
    weight_shared = weight_shared.reshape(2, experts, share, weight_shared.shape[2])
    weight_shared = reduce_step(weight_shared, "exp", 0)
    grad_sent, expert_rows, grad_gated, *kept = expert_pass(
        received, grad_rows, blocks_in, blocks_out, True
    )
    grad_sent, sum_part, weight_shared = lax.optimization_barrier(
        (grad_sent, sum_part, weight_shared)
    )
    shared_sum, first_sum = reduce_rows(sum_part)
    grad_back = exchange(grad_sent)
    grad_gated, first_sum = lax.optimization_barrier((grad_gated, first_sum))
    blocks = list(range(len(blocks_in)))
    shares = {}
    for mask in bits_of("hid")[:-1]:
        here, there = [r for r in blocks if not r & mask], [r for r in blocks if r & mask]
        made = outer_pass(
            received,
            grad_gated,
            [kept[r] for r in there],
            [kept[len(blocks_in) + r] for r in there],
            added=[part for kind in range(2) for part in (shares[kind, r] for r in there)]
            if shares
            else (),
        )
        shares = {
            (kind, r): swap(made[kind][there.index(r | mask)], "hid", mask)
            for kind in range(2)
            for r in here
        }
        blocks = here
    made_in, made_out = outer_pass(
        received,
        grad_gated,
        [kept[r] for r in blocks],
        [kept[len(blocks_in) + r] for r in blocks],
        added=[shares[kind, r] for kind in range(2) for r in blocks],
    )
    (kept_in, sent_in), (kept_out, sent_out) = made_in, made_out
    grad_back, expert_rows, sent_in, sent_out, weight_shared, shared_sum = (
        lax.optimization_barrier(
            (grad_back, expert_rows, sent_in, sent_out, weight_shared, shared_sum)
        )
    )
    shared_sum = reduce_more(shared_sum)
    weight_shared = spread_rest(weight_shared)
    moved_in, moved_out = swap(sent_in, "hid", far_mask), swap(sent_out, "hid", far_mask)
    back_rows = exchange(expert_rows)

    picked_grad = mat_prod(picks, grad_back)
    dots = jnp.sum(picked_grad[:, model_dim:], axis=1)
    picked_grad = picked_grad[:, :model_dim]
    grad_gap = (dots[:tokens] - dots[tokens:])[:, None] * gate_first * gate_second
    grad_logits = low(grad_gap * (first_hot - second_hot))
    grad_hidden = (
        prod_cols(grad_logits, router_weight)
        + shared_term
        + gate_first * picked_grad[:tokens]
        + gate_second * picked_grad[tokens:]
    ).reshape(item_count, SEQ, model_dim)
    grad_shift_two = jnp.sum(grad_hidden, axis=1)
    grad_scale_two = jnp.sum(grad_hidden * normed_two, axis=1)
    grad_residual = grad_result + normalize_back(
        normed_two, inverse_two, grad_hidden * (1.0 + scale_two)
    )
    grad_gate_one = jnp.sum(branch_one * grad_residual, axis=1)
    grad_branch_one = low((gate_one * grad_residual).reshape(tokens, model_dim))
    grad_attended = low(prod_cols(grad_branch_one, proj_weight))
    moved_in, moved_out, grad_attended = lax.optimization_barrier(
        (moved_in, moved_out, grad_attended)
    )
    grad_qkv = attend(attend_back_body, [qkv_rows, grad_attended], 3 * model_dim, score_scale)
    back_rows, shared_sum, weight_shared, grad_qkv = lax.optimization_barrier(
        (back_rows, shared_sum, weight_shared, grad_qkv)
    )
    padded = jnp.pad(grad_logits, ((0, 0), (0, -experts % 128)))
    dense, (grad_qkv,) = sum_hid(
        jnp.concatenate(
            [
                low(prod_rows(flat_one, grad_qkv)),
                low(prod_rows(attended_low, grad_branch_one)),
                low(prod_rows(hidden_two, padded)),
            ],
            axis=1,
        ),
        (grad_qkv,),
    )
    tail = dense[:1, :128]
    weight_expert_in = kept_in.astype(jnp.float32) + after(moved_in, tail).astype(jnp.float32)
    weight_expert_out = kept_out.astype(jnp.float32) + after(moved_out, tail).astype(jnp.float32)
    weight_shared = sum(part.astype(jnp.float32) for part in weight_shared)
    grad_hidden_one = prod_cols(grad_qkv, qkv_weight).reshape(item_count, SEQ, model_dim)
    grad_shift_one = jnp.sum(grad_hidden_one, axis=1)
    grad_scale_one = jnp.sum(grad_hidden_one * normed_one, axis=1)
    grad_input = grad_residual + normalize_back(
        normed_one, inverse_one, grad_hidden_one * (1.0 + scale_one)
    )
    grad_patches = low(grad_input.reshape(tokens, model_dim))
    picked = mat_prod(picks, back_rows)
    picked_first, picked_second = picked[:tokens], picked[tokens:]
    moe_out = gate_first * picked_first + gate_second * picked_second
    branch_two = (shared_sum + moe_out).reshape(item_count, SEQ, model_dim)
    output = low(residual_one + gate_two * branch_two).reshape(tokens, model_dim)
    grad_gate_two = jnp.sum(branch_two * grad_result, axis=1)
    counts_local = jnp.sum(
        first_hot * kept_first.astype(jnp.float32) + second_hot * kept_second.astype(jnp.float32),
        axis=0,
    )
    counts_rows = jnp.where(jnp.arange(item_count)[:, None] == 0, counts_local[None, :], 0.0)
    digits = jnp.stack(
        [timesteps >> 5, timesteps & 31, labels >> 5, labels & 31], axis=1
    ).astype(jnp.float32)
    item_rows = low(
        jnp.concatenate(
            [
                grad_shift_one,
                grad_scale_one,
                grad_gate_one,
                grad_shift_two,
                grad_scale_two,
                grad_gate_two,
                digits,
                counts_rows,
                jnp.zeros((item_count, -(experts + 4) % 128), jnp.float32),
            ],
            axis=1,
        )
    )
    item_rows, dense = gather_items(item_rows, dense)
    dense = sum_parts(exchange(dense))

    grad_modulate = item_rows[:, : 6 * model_dim]
    rest = item_rows[:, 6 * model_dim :].astype(jnp.float32)
    expert_counts = jnp.sum(rest[:, 4 : 4 + experts], axis=0)
    numbers = rest[:, 0:4:2] * 32.0 + rest[:, 1:4:2]
    freq_all, label_all, condition_all, silu_all = condition_of(
        numbers[:, 0].astype(jnp.int32),
        numbers[:, 1].astype(jnp.int32),
        time_weight,
        time_bias,
        class_table,
    )
    weight_ada = prod_rows(
        lax.dynamic_slice_in_dim(silu_all, place_exp * share, share, 1), grad_modulate
    )
    bias_ada = jnp.sum(grad_modulate.astype(jnp.float32), axis=0)
    grad_silu = prod_cols(grad_modulate, ada_weight)
    grad_condition = jax.vjp(jax.nn.silu, condition_all)[1](grad_silu)[0]
    bias_time = jnp.sum(grad_condition, axis=0)
    grad_condition_low = low(grad_condition)
    table_grad = prod_rows(label_all, grad_condition_low)
    freq_share = time_weight.shape[0] // experts
    weight_time = prod_rows(
        lax.dynamic_slice_in_dim(freq_all, place_exp * freq_share, freq_share, 1),
        grad_condition_low,
    )
    return (
        output,
        grad_patches,
        weight_time,
        bias_time,
        table_grad,
        weight_ada,
        bias_ada,
        dense[:, : 3 * model_dim],
        dense[:, 3 * model_dim : 4 * model_dim],
        dense[:, 4 * model_dim : 4 * model_dim + experts],
        weight_shared[0],
        weight_shared[1].T,
        weight_expert_in[None],
        weight_expert_out[None],
        expert_counts,
    )


def solution(mesh):
    placed = (
        P(("exp", "hid"), None),
        P(("exp", "hid"), None),
        P(("exp", "hid")),
        P(("exp", "hid")),
        P(("exp", "hid"), None),
        P(("exp", "hid"), None),
        P(),
        P(),
        P(),
        P(),
        P(),
        P(),
        P(),
        P(),
        P(None, "hid"),
        P("hid", None),
        P("exp", None, "hid"),
        P("exp", "hid", None),
    )
    return jax.shard_map(
        per_device,
        mesh=mesh,
        in_specs=placed,
        out_specs=(
            P(("exp", "hid"), None),
            P(("exp", "hid"), None),
            P("exp", None),
            P(),
            P(),
            P("exp", None),
            P(),
            P("exp", None),
            P("exp", None),
            P("exp", None),
            P("exp", "hid"),
            P("hid", "exp"),
            P("exp", None, "hid"),
            P("exp", "hid", None),
            P(),
        ),
        check_vma=False,
    )
```

```python
import functools
import math

import jax
import jax.numpy as jnp
from jax import lax
from jax.experimental import pallas as pl
from jax.experimental.pallas import tpu as pltpu
from jax.sharding import PartitionSpec as P

HEADS = 12
HDIM = 64
SEQ = 256
PIECES = 4


eps_norm = 1e-06
highest = lax.Precision.HIGHEST


def mat_prod(left_side, right_side):
    return jnp.dot(left_side, right_side, preferred_element_type=jnp.float32)


def prod_rows(left_side, right_side):
    return lax.dot_general(
        left_side, right_side, (((0,), (0,)), ((), ())), preferred_element_type=jnp.float32
    )


def prod_cols(left_side, right_side):
    return lax.dot_general(
        left_side, right_side, (((1,), (1,)), ((), ())), preferred_element_type=jnp.float32
    )


def sinus_table(timesteps, columns):
    half_cols = columns // 2
    freqs = jnp.exp(-math.log(10000.0) * jnp.arange(half_cols, dtype=jnp.float32) / half_cols)
    angles = timesteps.astype(jnp.float32)[:, None] * freqs[None, :]
    return jnp.concatenate([jnp.cos(angles), jnp.sin(angles)], axis=1)


def normalize(inputs):
    center = inputs - jnp.mean(inputs, axis=-1, keepdims=True)
    inverse = lax.rsqrt(jnp.mean(center * center, axis=-1, keepdims=True) + eps_norm)
    return (center * inverse, inverse)


def normalize_back(normed, inverse, grad_normed):
    return inverse * (
        grad_normed
        - jnp.mean(grad_normed, axis=-1, keepdims=True)
        - normed * jnp.mean(grad_normed * normed, axis=-1, keepdims=True)
    )


def pairs_of(size, mask):
    return [(index, index ^ mask) for index in range(size)]


def swap(values, axis, mask):
    return lax.ppermute(values, axis, pairs_of(lax.axis_size(axis), mask))


def low(values):
    return values.astype(jnp.bfloat16)


def bits_of(axis):
    masks = [1]
    while masks[-1] * 2 < lax.axis_size(axis):
        masks.append(masks[-1] * 2)
    return masks


def gather_hid(own, far):
    masks = bits_of("hid")
    blocks = {0: own, masks[-1]: far}
    for mask in reversed(masks[:-1]):
        for index in list(blocks):
            blocks[index ^ mask] = swap(blocks[index], "hid", mask)
    return [blocks[index] for index in range(lax.axis_size("hid"))]


def gather_rows(own):
    masks = bits_of("hid")
    rows, first = own, own
    for mask in reversed(masks[1:]):
        moved = swap(rows, "hid", mask)
        first = moved if rows is own else first
        rows = jnp.concatenate([rows, moved], axis=0)
    return (rows, swap(rows, "hid", masks[0])), first


def after(values, other):
    seen = other.reshape(-1)[0].astype(jnp.float32)
    return jnp.where(seen == seen, values, jnp.zeros_like(values))


def reduce_rows(halves):
    first = swap(halves[1], "hid", bits_of("hid")[0])
    return halves[0].astype(jnp.float32) + first.astype(jnp.float32), first


def reduce_more(rows):
    for mask in bits_of("hid")[1:-1]:
        half = rows.shape[0] // 2
        rows = rows[:half] + swap(low(rows[half:]), "hid", mask).astype(jnp.float32)
    half = rows.shape[0] // 2
    return rows[:half], swap(low(rows[half:]), "hid", bits_of("hid")[-1])


def reduce_step(values, axis, step):
    bit = (lax.axis_index(axis) >> step) & 1
    halves = values.reshape((values.shape[0], values.shape[1] // 2, 2) + values.shape[2:])
    kept = lax.dynamic_index_in_dim(halves, bit, 2, keepdims=False)
    sent = lax.dynamic_index_in_dim(halves, 1 - bit, 2, keepdims=False)
    return kept.astype(jnp.float32) + swap(low(sent), axis, 1 << step).astype(jnp.float32)


def spread_rest(values):
    left = values.shape[1]
    if left > 4:
        for step in range(1, len(bits_of("exp"))):
            values = reduce_step(values, "exp", step)
        return [values[:, 0]]
    place = lax.axis_index("exp") >> 1
    parts = [lax.dynamic_index_in_dim(values, place ^ mask, 1, keepdims=False) for mask in range(left)]
    return parts[:1] + [swap(low(parts[mask]), "exp", 2 * mask) for mask in range(1, left)]


def exchange(rows):
    return lax.all_to_all(rows, "exp", split_axis=0, concat_axis=0, tiled=True)


def join_hid(own):
    place = lax.axis_index("hid")
    for step, mask in reversed(list(enumerate(bits_of("hid")))):
        other = swap(own, "hid", mask)
        both = jnp.stack([own, other], axis=0)
        swapped = jnp.stack([other, own], axis=0)
        own = jnp.where((place >> step) & 1 == 0, both, swapped)
    depth = len(bits_of("hid"))
    own = jnp.transpose(own, tuple(reversed(range(depth))) + tuple(range(depth, own.ndim)))
    return own.reshape((-1,) + own.shape[depth + 1 :])


def gather_items(own, gate):
    count = own.shape[0]
    width = lax.axis_size("hid")
    rows, offsets = own, [0]
    for axis, weight in (("exp", width), ("hid", 1)):
        for mask in bits_of(axis):
            rows = jnp.concatenate([rows, swap(rows, axis, mask)], axis=0)
            offsets = offsets + [offset ^ (mask * weight) for offset in offsets]
        if axis == "exp":
            rows, gate = lax.optimization_barrier((rows, gate))
    place = lax.axis_index("exp") * width + lax.axis_index("hid")
    part = jnp.arange(len(offsets) * count, dtype=jnp.int32)
    source = (jnp.repeat(jnp.array(offsets, jnp.int32), count) ^ place) * count + part % count
    return low(mat_prod(low(source[None, :] == part[:, None]), rows)), gate


def sum_hid(partial, gates):
    size = lax.axis_size("exp")
    width = lax.axis_size("hid")
    columns = partial.shape[1]
    share = partial.shape[0] // (size * width)
    values = partial.reshape(size, width, share, columns)
    place = lax.axis_index("hid")
    masks = bits_of("hid")
    for step, mask in enumerate(masks):
        bit = (place >> step) & 1
        halves = values.reshape(size, values.shape[1] // 2, 2, share, columns)
        kept = lax.dynamic_index_in_dim(halves, bit, 2, keepdims=False)
        sent = low(lax.dynamic_index_in_dim(halves, 1 - bit, 2, keepdims=False))
        if mask == masks[-1]:
            sent, gates = lax.optimization_barrier((sent, gates))
        values = kept.astype(jnp.float32) + swap(sent, "hid", mask).astype(jnp.float32)
    return low(values).reshape(size * share, columns), gates


def sum_parts(values):
    size = lax.axis_size("exp")
    parts = values.reshape(size, values.shape[0] // size, values.shape[1])
    return join_hid(low(jnp.sum(parts.astype(jnp.float32), axis=0))).astype(jnp.float32)


SMALL_COST = pl.CostEstimate(flops=1000, bytes_accessed=1000, transcendentals=0)


def gelu_pair(pre):
    square = pre * pre
    scale = math.sqrt(2.0 / math.pi)
    bent = jnp.tanh(pre * (scale + (scale * 0.044715) * square))
    half = 0.5 + 0.5 * bent
    slope = half + (0.5 * pre) * (1.0 - bent * bent) * (scale + (3.0 * scale * 0.044715) * square)
    return pre * half, slope


def expert_body(block_count, width, gated, *refs):
    rows_ref, grads_ref = refs[0], refs[1]
    in_refs = refs[2 : 2 + block_count]
    out_refs = refs[2 + block_count : 2 + 2 * block_count]
    rest = refs[2 + 2 * block_count :]
    if gated:
        back_ref, sum_ref, scaled_ref = rest[:3]
        rest = rest[3:]
    else:
        back_ref, sum_ref = rest[:2]
        rest = rest[2:]
    act_refs, slope_refs = rest[:block_count], rest[block_count : 2 * block_count]
    pre_ref, hidden_ref, low_ref, sum_acc, back_acc = rest[2 * block_count :]
    count = rows_ref.shape[0]
    step = 32
    for index in range(block_count):
        pre_ref[...] = mat_prod(rows_ref[:, :width], in_refs[index][...])
        hidden_ref[...] = prod_cols(grads_ref[...], out_refs[index][...])

        def bend(place, carry, index=index):
            span = pl.ds(pl.multiple_of(place * step, step), step)
            act, slope = gelu_pair(pre_ref[span, :])
            back = hidden_ref[span, :] * slope
            act_refs[index][span, :] = low(act)
            if gated:
                low_ref[span, :] = low(back)
                gate = rows_ref[span, width : width + 128].astype(jnp.float32)
                slope_refs[index][span, :] = low(back * (gate[:, 0:1] + gate[:, 1:2]))
            else:
                slope_refs[index][span, :] = low(back)
            return carry

        lax.fori_loop(0, count // step, bend, 0)
        part_sum = mat_prod(act_refs[index][...], out_refs[index][...])
        sent = low_ref if gated else slope_refs[index]
        part_back = prod_cols(sent[...], in_refs[index][...])
        if index == 0:
            sum_acc[...] = part_sum
            back_acc[...] = part_back
        else:
            sum_acc[...] += part_sum
            back_acc[...] += part_back

    def finish(place, carry):
        span = pl.ds(pl.multiple_of(place * step, step), step)
        total = sum_acc[span, :]
        sum_ref[span, :] = low(total)
        back_ref[span, :width] = low(back_acc[span, :])
        if gated:
            grads = grads_ref[span, :].astype(jnp.float32)
            gate = rows_ref[span, width : width + 128].astype(jnp.float32)
            scaled_ref[span, :] = low(grads * (gate[:, 0:1] + gate[:, 1:2]))
            dots = jnp.sum(total * grads, axis=1, keepdims=True)
            high = low(dots).astype(jnp.float32)
            lane = lax.broadcasted_iota(jnp.int32, (step, 128), 1)
            back_ref[span, width : width + 128] = low(
                jnp.where(lane == 0, high, jnp.where(lane == 1, dots - high, 0.0))
            )
        return carry

    lax.fori_loop(0, count // step, finish, 0)


def expert_pass(rows, grads, blocks_in, blocks_out, gated):
    count, width = grads.shape
    hidden = blocks_in[0].shape[1]
    blocks = len(blocks_in)

    def shape(columns):
        return jax.ShapeDtypeStruct((count, columns), jnp.bfloat16)

    outs = [shape(rows.shape[1]), shape(width)] + ([shape(width)] if gated else [])
    outs += [shape(hidden)] * (2 * blocks)
    scratch = [
        pltpu.VMEM((count, hidden), jnp.float32),
        pltpu.VMEM((count, hidden), jnp.float32),
        pltpu.VMEM((count, hidden), jnp.bfloat16),
        pltpu.VMEM((count, width), jnp.float32),
        pltpu.VMEM((count, width), jnp.float32),
    ]
    return pl.pallas_call(
        functools.partial(expert_body, blocks, width, gated),
        out_shape=outs,
        scratch_shapes=scratch,
        cost_estimate=SMALL_COST,
        compiler_params=pltpu.CompilerParams(vmem_limit_bytes=56 * 1024 * 1024),
    )(rows, grads, *blocks_in, *blocks_out)


def outer_body(block_count, width, added, *refs):
    rows_ref, grads_ref = refs[0], refs[1]
    parts = [
        refs[2 + kind * block_count : 2 + (kind + 1) * block_count] for kind in range(6 if added else 4)
    ]
    act_refs, back_refs = parts[:2]
    in_refs, out_refs = parts[-2:]
    for index in range(block_count):
        first = prod_rows(rows_ref[:, :width], back_refs[index][...])
        second = prod_rows(act_refs[index][...], grads_ref[...])
        if added:
            first += parts[2][index][...].astype(jnp.float32)
            second += parts[3][index][...].astype(jnp.float32)
        in_refs[index][...] = low(first)
        out_refs[index][...] = low(second)


def outer_pass(rows, grads, acts, backs, added=()):
    width, hidden, blocks = grads.shape[1], acts[0].shape[1], len(acts)
    outs = [jax.ShapeDtypeStruct((width, hidden), jnp.bfloat16)] * blocks
    outs += [jax.ShapeDtypeStruct((hidden, width), jnp.bfloat16)] * blocks
    made = pl.pallas_call(
        functools.partial(outer_body, blocks, width, bool(added)),
        out_shape=outs,
        cost_estimate=SMALL_COST,
        compiler_params=pltpu.CompilerParams(vmem_limit_bytes=56 * 1024 * 1024),
    )(rows, grads, *acts, *backs, *added)
    return made[:blocks], made[blocks:]


def shared_body(rows_a, rows_b, grads_a, grads_b, act_a, act_b, back_a, back_b, out_ref):
    out_ref[0] = low(prod_rows(rows_a[...], back_a[...]) + prod_rows(rows_b[...], back_b[...]))
    out_ref[1] = low(prod_rows(grads_a[...], act_a[...]) + prod_rows(grads_b[...], act_b[...]))


def shared_outer(*arrays):
    return pl.pallas_call(
        shared_body,
        out_shape=jax.ShapeDtypeStruct((2, arrays[0].shape[1], arrays[4].shape[1]), jnp.bfloat16),
        cost_estimate=SMALL_COST,
        compiler_params=pltpu.CompilerParams(vmem_limit_bytes=56 * 1024 * 1024),
    )(*arrays)


def head_weights(queries, key_rows, score_scale):
    scores = prod_cols(queries, key_rows) * score_scale
    raised = jnp.exp(scores - jnp.max(scores, axis=1, keepdims=True))
    return raised / jnp.sum(raised, axis=1, keepdims=True)


def pair_spans(pair, width):
    return [pl.ds(pl.multiple_of(part * width + pair * 128, 128), 128) for part in range(3)]


def attend_body(score_scale, rows_ref, out_ref):
    width = out_ref.shape[1]
    lane = lax.broadcasted_iota(jnp.int32, (out_ref.shape[0], 128), 1)

    def step(pair, carry):
        at_q, at_k, at_v = pair_spans(pair, width)
        queries, keys, values = rows_ref[:, at_q], rows_ref[:, at_k], rows_ref[:, at_v]
        sides = []
        for side in range(2):
            mine = (lane >= side * HDIM) & (lane < (side + 1) * HDIM)
            weights = head_weights(jnp.where(mine, queries, 0), keys, score_scale)
            sides.append(mat_prod(low(weights), values))
        out_ref[:, at_q] = low(jnp.where(lane < HDIM, sides[0], sides[1]))
        return carry

    lax.fori_loop(0, width // 128, step, 0)


def attend_back_body(score_scale, rows_ref, grad_ref, out_ref):
    width = grad_ref.shape[1]
    lane = lax.broadcasted_iota(jnp.int32, (grad_ref.shape[0], 128), 1)

    def step(pair, carry):
        at_q, at_k, at_v = pair_spans(pair, width)
        queries, keys, values = rows_ref[:, at_q], rows_ref[:, at_k], rows_ref[:, at_v]
        grads = grad_ref[:, at_q]
        to_q, to_k, to_v = [], [], []
        for side in range(2):
            mine = (lane >= side * HDIM) & (lane < (side + 1) * HDIM)
            head_queries, head_grads = jnp.where(mine, queries, 0), jnp.where(mine, grads, 0)
            weights = head_weights(head_queries, keys, score_scale)
            to_v.append(prod_rows(low(weights), head_grads))
            probs = prod_cols(head_grads, values)
            inner = jnp.sum(weights * probs, axis=1, keepdims=True)
            scores = low(weights * (probs - inner) * score_scale)
            to_q.append(mat_prod(scores, keys))
            to_k.append(prod_rows(scores, head_queries))
        out_ref[:, at_q] = low(jnp.where(lane < HDIM, to_q[0], to_q[1]))
        out_ref[:, at_k] = low(to_k[0] + to_k[1])
        out_ref[:, at_v] = low(to_v[0] + to_v[1])
        return carry

    lax.fori_loop(0, width // 128, step, 0)


def attend(body, arrays, columns, score_scale):
    rows = arrays[0].shape[0]
    return pl.pallas_call(
        functools.partial(body, score_scale),
        grid=(rows // SEQ,),
        in_specs=[pl.BlockSpec((SEQ, array.shape[1]), lambda item: (item, 0)) for array in arrays],
        out_specs=pl.BlockSpec((SEQ, columns), lambda item: (item, 0)),
        out_shape=jax.ShapeDtypeStruct((rows, columns), jnp.bfloat16),
        cost_estimate=SMALL_COST,
    )(*arrays)


def condition_of(timesteps, labels, time_weight, time_bias, class_table):
    freq_emb = low(sinus_table(timesteps, time_weight.shape[0]))
    label_hot = low(
        labels[:, None] == jnp.arange(class_table.shape[0], dtype=jnp.int32)[None, :]
    )
    condition = mat_prod(freq_emb, time_weight) + time_bias + mat_prod(label_hot, class_table)
    return freq_emb, label_hot, condition, low(jax.nn.silu(condition))


def per_device(
    patches,
    cotangent,
    timesteps,
    labels,
    routes,
    slot_index,
    time_weight,
    time_bias,
    class_table,
    ada_weight,
    ada_bias,
    qkv_weight,
    proj_weight,
    router_weight,
    shared_in,
    shared_out,
    expert_in,
    expert_out,
):
    tokens, model_dim = patches.shape
    item_count = timesteps.shape[0]
    experts = lax.axis_size("exp")
    place_exp = lax.axis_index("exp")
    capacity = 9 * tokens // (4 * experts)
    slots_all = experts * capacity
    score_scale = 1.0 / math.sqrt(HDIM)

    own_in, own_out = expert_in[0], expert_out[0]
    far_mask = bits_of("hid")[-1]
    far_in = swap(own_in, "hid", far_mask)

    freq_emb, label_hot, condition, silu_cond = condition_of(
        timesteps, labels, time_weight, time_bias, class_table
    )
    modulate = mat_prod(silu_cond, ada_weight) + ada_bias
    shift_one, scale_one, gate_one, shift_two, scale_two, gate_two = [
        modulate[:, None, block_index * model_dim : (block_index + 1) * model_dim]
        for block_index in range(6)
    ]
    grad_result = cotangent.astype(jnp.float32).reshape(item_count, SEQ, model_dim)
    grad_branch = (gate_two * grad_result).reshape(tokens, model_dim)
    grad_branch_low = low(grad_branch)

    first_route, second_route = routes[:, 0:1], routes[:, 1:2]
    kept_first = slot_index[:, 0:1] < capacity
    kept_second = slot_index[:, 1:2] < capacity
    slot_ids = jnp.arange(slots_all, dtype=jnp.int32)[None, :]
    dispatch_first = low(
        (first_route * capacity + slot_index[:, 0:1] == slot_ids) & kept_first
    )
    dispatch_second = low(
        (second_route * capacity + slot_index[:, 1:2] == slot_ids) & kept_second
    )
    dispatch_both = dispatch_first + dispatch_second
    picks = jnp.concatenate([dispatch_first, dispatch_second], axis=0)
    grad_rows = exchange(low(prod_rows(dispatch_both, grad_branch_low)))
    grad_tokens, _ = gather_rows(grad_branch_low)

    residual = patches.astype(jnp.float32).reshape(item_count, SEQ, model_dim)
    normed_one, inverse_one = normalize(residual)
    flat_one = low(normed_one * (1.0 + scale_one) + shift_one).reshape(tokens, model_dim)
    qkv_rows = low(mat_prod(flat_one, qkv_weight))
    qkv_rows, far_in = lax.optimization_barrier((qkv_rows, far_in))
    attended_low = attend(attend_body, [qkv_rows], model_dim, score_scale)
    branch_one = mat_prod(attended_low, proj_weight).reshape(item_count, SEQ, model_dim)
    residual_one = residual + gate_one * branch_one
    normed_two, inverse_two = normalize(residual_one)
    hidden_two = low(normed_two * (1.0 + scale_two) + shift_two).reshape(tokens, model_dim)
    logits = mat_prod(hidden_two, router_weight)
    expert_ids = jnp.arange(experts, dtype=jnp.int32)[None, :]
    first_hot = (first_route == expert_ids).astype(jnp.float32)
    second_hot = (second_route == expert_ids).astype(jnp.float32)
    logit_gap = jnp.sum(logits * first_hot, axis=1) - jnp.sum(logits * second_hot, axis=1)
    gate_first = jax.nn.sigmoid(logit_gap)[:, None]
    gate_second = 1.0 - gate_first

    lane = jnp.arange(128, dtype=jnp.int32)[None, :]

    def gate_lanes(gate):
        high = low(gate).astype(jnp.float32)
        return low(jnp.where(lane == 0, high, jnp.where(lane == 1, gate - high, 0.0)))

    carried = jnp.concatenate(
        [
            jnp.concatenate([hidden_two, hidden_two], axis=0),
            jnp.concatenate([gate_lanes(gate_first), gate_lanes(gate_second)], axis=0),
        ],
        axis=1,
    )
    sent_rows, grad_rows = lax.optimization_barrier((low(prod_rows(picks, carried)), grad_rows))
    received = exchange(sent_rows)
    blocks_in = gather_hid(own_in, far_in)
    tokens_all, first_tokens = gather_rows(hidden_two)
    far_out = swap(after(own_out, first_tokens[:1, :128]), "hid", far_mask)
    blocks_out = gather_hid(own_out, far_out)

    halves = [
        expert_pass(rows, grads, [shared_in], [shared_out], False)
        for rows, grads in zip(tokens_all, grad_tokens)
    ]
    term_part, sum_part, act_shared, back_shared = zip(*halves)
    near_term, far_term = reduce_more(reduce_rows(term_part)[0])
    shared_term = near_term + far_term.astype(jnp.float32)
    weight_shared = shared_outer(*tokens_all, *grad_tokens, *act_shared, *back_shared)

    received, weight_shared = lax.optimization_barrier((received, weight_shared))
    share = model_dim // experts
    weight_shared = weight_shared.reshape(2, experts, share, weight_shared.shape[2])
    weight_shared = reduce_step(weight_shared, "exp", 0)
    grad_sent, expert_rows, grad_gated, *kept = expert_pass(
        received, grad_rows, blocks_in, blocks_out, True
    )
    grad_sent, sum_part, weight_shared = lax.optimization_barrier(
        (grad_sent, sum_part, weight_shared)
    )
    shared_sum, first_sum = reduce_rows(sum_part)
    grad_back = exchange(grad_sent)
    grad_gated, first_sum = lax.optimization_barrier((grad_gated, first_sum))
    blocks = list(range(len(blocks_in)))
    shares = {}
    for mask in bits_of("hid")[:-1]:
        here, there = [r for r in blocks if not r & mask], [r for r in blocks if r & mask]
        made = outer_pass(
            received,
            grad_gated,
            [kept[r] for r in there],
            [kept[len(blocks_in) + r] for r in there],
            added=[part for kind in range(2) for part in (shares[kind, r] for r in there)]
            if shares
            else (),
        )
        shares = {
            (kind, r): swap(made[kind][there.index(r | mask)], "hid", mask)
            for kind in range(2)
            for r in here
        }
        blocks = here
    made_in, made_out = outer_pass(
        received,
        grad_gated,
        [kept[r] for r in blocks],
        [kept[len(blocks_in) + r] for r in blocks],
        added=[shares[kind, r] for kind in range(2) for r in blocks],
    )
    (kept_in, sent_in), (kept_out, sent_out) = made_in, made_out
    near_sum, far_sum = reduce_more(shared_sum)
    grad_back, expert_rows, sent_in, sent_out, weight_shared, far_sum = lax.optimization_barrier(
        (grad_back, expert_rows, sent_in, sent_out, weight_shared, far_sum)
    )
    shared_sum = near_sum + far_sum.astype(jnp.float32)
    moved_in = swap(sent_in, "hid", far_mask)
    cut = sent_out.shape[0] // PIECES
    moved_out, last = [], moved_in
    for piece in range(PIECES):
        last, part = lax.optimization_barrier((last, sent_out[piece * cut : (piece + 1) * cut]))
        if piece == 0:
            moved_in = last
        else:
            moved_out[-1] = last
        last = swap(part, "hid", far_mask)
        moved_out.append(last)
    weight_shared = spread_rest(weight_shared)
    back_rows = exchange(expert_rows)

    picked_grad = mat_prod(picks, grad_back)
    dots = jnp.sum(picked_grad[:, model_dim:], axis=1)
    picked_grad = picked_grad[:, :model_dim]
    grad_gap = (dots[:tokens] - dots[tokens:])[:, None] * gate_first * gate_second
    grad_logits = low(grad_gap * (first_hot - second_hot))
    grad_hidden = (
        prod_cols(grad_logits, router_weight)
        + shared_term
        + gate_first * picked_grad[:tokens]
        + gate_second * picked_grad[tokens:]
    ).reshape(item_count, SEQ, model_dim)
    grad_shift_two = jnp.sum(grad_hidden, axis=1)
    grad_scale_two = jnp.sum(grad_hidden * normed_two, axis=1)
    grad_residual = grad_result + normalize_back(
        normed_two, inverse_two, grad_hidden * (1.0 + scale_two)
    )
    grad_gate_one = jnp.sum(branch_one * grad_residual, axis=1)
    grad_branch_one = low((gate_one * grad_residual).reshape(tokens, model_dim))
    grad_attended = low(prod_cols(grad_branch_one, proj_weight))
    moved_in, grad_attended = lax.optimization_barrier((moved_in, grad_attended))
    grad_qkv = attend(attend_back_body, [qkv_rows, grad_attended], 3 * model_dim, score_scale)
    back_rows, shared_sum, weight_shared, grad_qkv = lax.optimization_barrier(
        (back_rows, shared_sum, weight_shared, grad_qkv)
    )
    padded = jnp.pad(grad_logits, ((0, 0), (0, -experts % 128)))
    dense, (moved_out,) = sum_hid(
        jnp.concatenate(
            [
                low(prod_rows(flat_one, grad_qkv)),
                low(prod_rows(attended_low, grad_branch_one)),
                low(prod_rows(hidden_two, padded)),
            ],
            axis=1,
        ),
        (moved_out,),
    )
    tail = dense[:1, :128]
    moved_out = jnp.concatenate(moved_out, axis=0)
    weight_expert_in = kept_in.astype(jnp.float32) + after(moved_in, tail).astype(jnp.float32)
    weight_expert_out = kept_out.astype(jnp.float32) + after(moved_out, tail).astype(jnp.float32)
    weight_shared = sum(part.astype(jnp.float32) for part in weight_shared)
    grad_hidden_one = prod_cols(grad_qkv, qkv_weight).reshape(item_count, SEQ, model_dim)
    grad_shift_one = jnp.sum(grad_hidden_one, axis=1)
    grad_scale_one = jnp.sum(grad_hidden_one * normed_one, axis=1)
    grad_input = grad_residual + normalize_back(
        normed_one, inverse_one, grad_hidden_one * (1.0 + scale_one)
    )
    grad_patches = low(grad_input.reshape(tokens, model_dim))
    picked = mat_prod(picks, back_rows)
    picked_first, picked_second = picked[:tokens], picked[tokens:]
    moe_out = gate_first * picked_first + gate_second * picked_second
    branch_two = (shared_sum + moe_out).reshape(item_count, SEQ, model_dim)
    output = low(residual_one + gate_two * branch_two).reshape(tokens, model_dim)
    grad_gate_two = jnp.sum(branch_two * grad_result, axis=1)
    counts_local = jnp.sum(
        first_hot * kept_first.astype(jnp.float32) + second_hot * kept_second.astype(jnp.float32),
        axis=0,
    )
    counts_rows = jnp.where(jnp.arange(item_count)[:, None] == 0, counts_local[None, :], 0.0)
    digits = jnp.stack(
        [timesteps >> 5, timesteps & 31, labels >> 5, labels & 31], axis=1
    ).astype(jnp.float32)
    item_rows = low(
        jnp.concatenate(
            [
                grad_shift_one,
                grad_scale_one,
                grad_gate_one,
                grad_shift_two,
                grad_scale_two,
                grad_gate_two,
                digits,
                counts_rows,
                jnp.zeros((item_count, -(experts + 4) % 128), jnp.float32),
            ],
            axis=1,
        )
    )
    item_rows, dense = gather_items(item_rows, dense)
    dense = sum_parts(exchange(dense))

    grad_modulate = item_rows[:, : 6 * model_dim]
    rest = item_rows[:, 6 * model_dim :].astype(jnp.float32)
    expert_counts = jnp.sum(rest[:, 4 : 4 + experts], axis=0)
    numbers = rest[:, 0:4:2] * 32.0 + rest[:, 1:4:2]
    freq_all, label_all, condition_all, silu_all = condition_of(
        numbers[:, 0].astype(jnp.int32),
        numbers[:, 1].astype(jnp.int32),
        time_weight,
        time_bias,
        class_table,
    )
    weight_ada = prod_rows(
        lax.dynamic_slice_in_dim(silu_all, place_exp * share, share, 1), grad_modulate
    )
    bias_ada = jnp.sum(grad_modulate.astype(jnp.float32), axis=0)
    grad_silu = prod_cols(grad_modulate, ada_weight)
    grad_condition = jax.vjp(jax.nn.silu, condition_all)[1](grad_silu)[0]
    bias_time = jnp.sum(grad_condition, axis=0)
    grad_condition_low = low(grad_condition)
    table_grad = prod_rows(label_all, grad_condition_low)
    freq_share = time_weight.shape[0] // experts
    weight_time = prod_rows(
        lax.dynamic_slice_in_dim(freq_all, place_exp * freq_share, freq_share, 1),
        grad_condition_low,
    )
    return (
        output,
        grad_patches,
        weight_time,
        bias_time,
        table_grad,
        weight_ada,
        bias_ada,
        dense[:, : 3 * model_dim],
        dense[:, 3 * model_dim : 4 * model_dim],
        dense[:, 4 * model_dim : 4 * model_dim + experts],
        weight_shared[0],
        weight_shared[1].T,
        weight_expert_in[None],
        weight_expert_out[None],
        expert_counts,
    )


def solution(mesh):
    placed = (
        P(("exp", "hid"), None),
        P(("exp", "hid"), None),
        P(("exp", "hid")),
        P(("exp", "hid")),
        P(("exp", "hid"), None),
        P(("exp", "hid"), None),
        P(),
        P(),
        P(),
        P(),
        P(),
        P(),
        P(),
        P(),
        P(None, "hid"),
        P("hid", None),
        P("exp", None, "hid"),
        P("exp", "hid", None),
    )
    return jax.shard_map(
        per_device,
        mesh=mesh,
        in_specs=placed,
        out_specs=(
            P(("exp", "hid"), None),
            P(("exp", "hid"), None),
            P("exp", None),
            P(),
            P(),
            P("exp", None),
            P(),
            P("exp", None),
            P("exp", None),
            P("exp", None),
            P("exp", "hid"),
            P("hid", "exp"),
            P("exp", None, "hid"),
            P("exp", "hid", None),
            P(),
        ),
        check_vma=False,
    )
```

```python
import functools
import math

import jax
import jax.numpy as jnp
from jax import lax
from jax.experimental import pallas as pl
from jax.experimental.pallas import tpu as pltpu
from jax.sharding import PartitionSpec as P

HEADS = 12
HDIM = 64
SEQ = 256
PIECES = 4


eps_norm = 1e-06
highest = lax.Precision.HIGHEST


def mat_prod(left_side, right_side):
    return jnp.dot(left_side, right_side, preferred_element_type=jnp.float32)


def prod_rows(left_side, right_side):
    return lax.dot_general(
        left_side, right_side, (((0,), (0,)), ((), ())), preferred_element_type=jnp.float32
    )


def prod_cols(left_side, right_side):
    return lax.dot_general(
        left_side, right_side, (((1,), (1,)), ((), ())), preferred_element_type=jnp.float32
    )


def sinus_table(timesteps, columns):
    half_cols = columns // 2
    freqs = jnp.exp(-math.log(10000.0) * jnp.arange(half_cols, dtype=jnp.float32) / half_cols)
    angles = timesteps.astype(jnp.float32)[:, None] * freqs[None, :]
    return jnp.concatenate([jnp.cos(angles), jnp.sin(angles)], axis=1)


def normalize(inputs):
    center = inputs - jnp.mean(inputs, axis=-1, keepdims=True)
    inverse = lax.rsqrt(jnp.mean(center * center, axis=-1, keepdims=True) + eps_norm)
    return (center * inverse, inverse)


def normalize_back(normed, inverse, grad_normed):
    return inverse * (
        grad_normed
        - jnp.mean(grad_normed, axis=-1, keepdims=True)
        - normed * jnp.mean(grad_normed * normed, axis=-1, keepdims=True)
    )


def pairs_of(size, mask):
    return [(index, index ^ mask) for index in range(size)]


def swap(values, axis, mask):
    return lax.ppermute(values, axis, pairs_of(lax.axis_size(axis), mask))


def low(values):
    return values.astype(jnp.bfloat16)


def bits_of(axis):
    masks = [1]
    while masks[-1] * 2 < lax.axis_size(axis):
        masks.append(masks[-1] * 2)
    return masks


def gather_hid(own, far):
    masks = bits_of("hid")
    blocks = {0: own, masks[-1]: far}
    for mask in reversed(masks[:-1]):
        for index in list(blocks):
            blocks[index ^ mask] = swap(blocks[index], "hid", mask)
    return [blocks[index] for index in range(lax.axis_size("hid"))]


def gather_rows(own):
    masks = bits_of("hid")
    rows, first = own, own
    for mask in reversed(masks[1:]):
        moved = swap(rows, "hid", mask)
        first = moved if rows is own else first
        rows = jnp.concatenate([rows, moved], axis=0)
    return (rows, swap(rows, "hid", masks[0])), first


def after(values, other):
    seen = other.reshape(-1)[0].astype(jnp.float32)
    return jnp.where(seen == seen, values, jnp.zeros_like(values))


def reduce_rows(halves):
    first = swap(halves[1], "hid", bits_of("hid")[0])
    return halves[0].astype(jnp.float32) + first.astype(jnp.float32), first


def reduce_more(rows):
    for mask in bits_of("hid")[1:-1]:
        half = rows.shape[0] // 2
        rows = rows[:half] + swap(low(rows[half:]), "hid", mask).astype(jnp.float32)
    half = rows.shape[0] // 2
    return rows[:half], swap(low(rows[half:]), "hid", bits_of("hid")[-1])


def reduce_step(values, axis, step):
    bit = (lax.axis_index(axis) >> step) & 1
    halves = values.reshape((values.shape[0], values.shape[1] // 2, 2) + values.shape[2:])
    kept = lax.dynamic_index_in_dim(halves, bit, 2, keepdims=False)
    sent = lax.dynamic_index_in_dim(halves, 1 - bit, 2, keepdims=False)
    return kept.astype(jnp.float32) + swap(low(sent), axis, 1 << step).astype(jnp.float32)


def spread_rest(values):
    left = values.shape[1]
    if left > 4:
        for step in range(1, len(bits_of("exp"))):
            values = reduce_step(values, "exp", step)
        return [values[:, 0]]
    place = lax.axis_index("exp") >> 1
    parts = [lax.dynamic_index_in_dim(values, place ^ mask, 1, keepdims=False) for mask in range(left)]
    return parts[:1] + [swap(low(parts[mask]), "exp", 2 * mask) for mask in range(1, left)]


def exchange(rows):
    return lax.all_to_all(rows, "exp", split_axis=0, concat_axis=0, tiled=True)


def join_hid(own):
    place = lax.axis_index("hid")
    for step, mask in reversed(list(enumerate(bits_of("hid")))):
        other = swap(own, "hid", mask)
        both = jnp.stack([own, other], axis=0)
        swapped = jnp.stack([other, own], axis=0)
        own = jnp.where((place >> step) & 1 == 0, both, swapped)
    depth = len(bits_of("hid"))
    own = jnp.transpose(own, tuple(reversed(range(depth))) + tuple(range(depth, own.ndim)))
    return own.reshape((-1,) + own.shape[depth + 1 :])


def gather_items(own, gate):
    count = own.shape[0]
    width = lax.axis_size("hid")
    rows, offsets = own, [0]
    for axis, weight in (("exp", width), ("hid", 1)):
        for mask in bits_of(axis):
            rows = jnp.concatenate([rows, swap(rows, axis, mask)], axis=0)
            offsets = offsets + [offset ^ (mask * weight) for offset in offsets]
        if axis == "exp":
            rows, gate = lax.optimization_barrier((rows, gate))
    place = lax.axis_index("exp") * width + lax.axis_index("hid")
    part = jnp.arange(len(offsets) * count, dtype=jnp.int32)
    source = (jnp.repeat(jnp.array(offsets, jnp.int32), count) ^ place) * count + part % count
    return low(mat_prod(low(source[None, :] == part[:, None]), rows)), gate


def sum_hid(partial, gates):
    size = lax.axis_size("exp")
    width = lax.axis_size("hid")
    columns = partial.shape[1]
    share = partial.shape[0] // (size * width)
    values = partial.reshape(size, width, share, columns)
    place = lax.axis_index("hid")
    masks = bits_of("hid")
    for step, mask in enumerate(masks):
        bit = (place >> step) & 1
        halves = values.reshape(size, values.shape[1] // 2, 2, share, columns)
        kept = lax.dynamic_index_in_dim(halves, bit, 2, keepdims=False)
        sent = low(lax.dynamic_index_in_dim(halves, 1 - bit, 2, keepdims=False))
        if mask == masks[-1]:
            sent, gates = lax.optimization_barrier((sent, gates))
        values = kept.astype(jnp.float32) + swap(sent, "hid", mask).astype(jnp.float32)
    return low(values).reshape(size * share, columns), gates


def sum_parts(values):
    size = lax.axis_size("exp")
    parts = values.reshape(size, values.shape[0] // size, values.shape[1])
    return join_hid(low(jnp.sum(parts.astype(jnp.float32), axis=0))).astype(jnp.float32)


SMALL_COST = pl.CostEstimate(flops=1000, bytes_accessed=1000, transcendentals=0)


def gelu_pair(pre):
    square = pre * pre
    scale = math.sqrt(2.0 / math.pi)
    bent = jnp.tanh(pre * (scale + (scale * 0.044715) * square))
    half = 0.5 + 0.5 * bent
    slope = half + (0.5 * pre) * (1.0 - bent * bent) * (scale + (3.0 * scale * 0.044715) * square)
    return pre * half, slope


def expert_body(block_count, width, gated, *refs):
    rows_ref, grads_ref = refs[0], refs[1]
    in_refs = refs[2 : 2 + block_count]
    out_refs = refs[2 + block_count : 2 + 2 * block_count]
    rest = refs[2 + 2 * block_count :]
    if gated:
        back_ref, sum_ref, scaled_ref = rest[:3]
        rest = rest[3:]
    else:
        back_ref, sum_ref = rest[:2]
        rest = rest[2:]
    act_refs, slope_refs = rest[:block_count], rest[block_count : 2 * block_count]
    pre_ref, hidden_ref, low_ref, sum_acc, back_acc = rest[2 * block_count :]
    count = rows_ref.shape[0]
    step = 64
    for index in range(block_count):
        pre_ref[...] = mat_prod(rows_ref[:, :width], in_refs[index][...])
        hidden_ref[...] = prod_cols(grads_ref[...], out_refs[index][...])

        def bend(place, carry, index=index):
            span = pl.ds(pl.multiple_of(place * step, step), step)
            act, slope = gelu_pair(pre_ref[span, :])
            back = hidden_ref[span, :] * slope
            act_refs[index][span, :] = low(act)
            if gated:
                low_ref[span, :] = low(back)
                gate = rows_ref[span, width : width + 128].astype(jnp.float32)
                slope_refs[index][span, :] = low(back * (gate[:, 0:1] + gate[:, 1:2]))
            else:
                slope_refs[index][span, :] = low(back)
            return carry

        lax.fori_loop(0, count // step, bend, 0)
        part_sum = mat_prod(act_refs[index][...], out_refs[index][...])
        sent = low_ref if gated else slope_refs[index]
        part_back = prod_cols(sent[...], in_refs[index][...])
        if index == 0:
            sum_acc[...] = part_sum
            back_acc[...] = part_back
        else:
            sum_acc[...] += part_sum
            back_acc[...] += part_back

    def finish(place, carry):
        span = pl.ds(pl.multiple_of(place * step, step), step)
        total = sum_acc[span, :]
        sum_ref[span, :] = low(total)
        back_ref[span, :width] = low(back_acc[span, :])
        if gated:
            grads = grads_ref[span, :].astype(jnp.float32)
            gate = rows_ref[span, width : width + 128].astype(jnp.float32)
            scaled_ref[span, :] = low(grads * (gate[:, 0:1] + gate[:, 1:2]))
            dots = jnp.sum(total * grads, axis=1, keepdims=True)
            high = low(dots).astype(jnp.float32)
            lane = lax.broadcasted_iota(jnp.int32, (step, 128), 1)
            back_ref[span, width : width + 128] = low(
                jnp.where(lane == 0, high, jnp.where(lane == 1, dots - high, 0.0))
            )
        return carry

    lax.fori_loop(0, count // step, finish, 0)


def expert_pass(rows, grads, blocks_in, blocks_out, gated):
    count, width = grads.shape
    hidden = blocks_in[0].shape[1]
    blocks = len(blocks_in)

    def shape(columns):
        return jax.ShapeDtypeStruct((count, columns), jnp.bfloat16)

    outs = [shape(rows.shape[1]), shape(width)] + ([shape(width)] if gated else [])
    outs += [shape(hidden)] * (2 * blocks)
    scratch = [
        pltpu.VMEM((count, hidden), jnp.float32),
        pltpu.VMEM((count, hidden), jnp.float32),
        pltpu.VMEM((count, hidden), jnp.bfloat16),
        pltpu.VMEM((count, width), jnp.float32),
        pltpu.VMEM((count, width), jnp.float32),
    ]
    return pl.pallas_call(
        functools.partial(expert_body, blocks, width, gated),
        out_shape=outs,
        scratch_shapes=scratch,
        cost_estimate=SMALL_COST,
        compiler_params=pltpu.CompilerParams(vmem_limit_bytes=56 * 1024 * 1024),
    )(rows, grads, *blocks_in, *blocks_out)


def outer_body(block_count, width, added, *refs):
    rows_ref, grads_ref = refs[0], refs[1]
    parts = [
        refs[2 + kind * block_count : 2 + (kind + 1) * block_count] for kind in range(6 if added else 4)
    ]
    act_refs, back_refs = parts[:2]
    in_refs, out_refs = parts[-2:]
    for index in range(block_count):
        first = prod_rows(rows_ref[:, :width], back_refs[index][...])
        second = prod_rows(act_refs[index][...], grads_ref[...])
        if added:
            first += parts[2][index][...].astype(jnp.float32)
            second += parts[3][index][...].astype(jnp.float32)
        in_refs[index][...] = low(first)
        out_refs[index][...] = low(second)


def outer_pass(rows, grads, acts, backs, added=()):
    width, hidden, blocks = grads.shape[1], acts[0].shape[1], len(acts)
    outs = [jax.ShapeDtypeStruct((width, hidden), jnp.bfloat16)] * blocks
    outs += [jax.ShapeDtypeStruct((hidden, width), jnp.bfloat16)] * blocks
    made = pl.pallas_call(
        functools.partial(outer_body, blocks, width, bool(added)),
        out_shape=outs,
        cost_estimate=SMALL_COST,
        compiler_params=pltpu.CompilerParams(vmem_limit_bytes=56 * 1024 * 1024),
    )(rows, grads, *acts, *backs, *added)
    return made[:blocks], made[blocks:]


def shared_body(rows_a, rows_b, grads_a, grads_b, act_a, act_b, back_a, back_b, out_ref):
    out_ref[0] = low(prod_rows(rows_a[...], back_a[...]) + prod_rows(rows_b[...], back_b[...]))
    out_ref[1] = low(prod_rows(grads_a[...], act_a[...]) + prod_rows(grads_b[...], act_b[...]))


def shared_outer(*arrays):
    return pl.pallas_call(
        shared_body,
        out_shape=jax.ShapeDtypeStruct((2, arrays[0].shape[1], arrays[4].shape[1]), jnp.bfloat16),
        cost_estimate=SMALL_COST,
        compiler_params=pltpu.CompilerParams(vmem_limit_bytes=56 * 1024 * 1024),
    )(*arrays)


def head_weights(queries, key_rows, score_scale):
    scores = prod_cols(queries, key_rows) * score_scale
    raised = jnp.exp(scores - jnp.max(scores, axis=1, keepdims=True))
    return raised / jnp.sum(raised, axis=1, keepdims=True)


def pair_spans(pair, width):
    return [pl.ds(pl.multiple_of(part * width + pair * 128, 128), 128) for part in range(3)]


def attend_body(score_scale, rows_ref, out_ref):
    width = out_ref.shape[1]
    lane = lax.broadcasted_iota(jnp.int32, (out_ref.shape[0], 128), 1)

    def step(pair, carry):
        at_q, at_k, at_v = pair_spans(pair, width)
        queries, keys, values = rows_ref[:, at_q], rows_ref[:, at_k], rows_ref[:, at_v]
        sides = []
        for side in range(2):
            mine = (lane >= side * HDIM) & (lane < (side + 1) * HDIM)
            weights = head_weights(jnp.where(mine, queries, 0), keys, score_scale)
            sides.append(mat_prod(low(weights), values))
        out_ref[:, at_q] = low(jnp.where(lane < HDIM, sides[0], sides[1]))
        return carry

    lax.fori_loop(0, width // 128, step, 0)


def attend_back_body(score_scale, rows_ref, grad_ref, out_ref):
    width = grad_ref.shape[1]
    lane = lax.broadcasted_iota(jnp.int32, (grad_ref.shape[0], 128), 1)

    def step(pair, carry):
        at_q, at_k, at_v = pair_spans(pair, width)
        queries, keys, values = rows_ref[:, at_q], rows_ref[:, at_k], rows_ref[:, at_v]
        grads = grad_ref[:, at_q]
        to_q, to_k, to_v = [], [], []
        for side in range(2):
            mine = (lane >= side * HDIM) & (lane < (side + 1) * HDIM)
            head_queries, head_grads = jnp.where(mine, queries, 0), jnp.where(mine, grads, 0)
            weights = head_weights(head_queries, keys, score_scale)
            to_v.append(prod_rows(low(weights), head_grads))
            probs = prod_cols(head_grads, values)
            inner = jnp.sum(weights * probs, axis=1, keepdims=True)
            scores = low(weights * (probs - inner) * score_scale)
            to_q.append(mat_prod(scores, keys))
            to_k.append(prod_rows(scores, head_queries))
        out_ref[:, at_q] = low(jnp.where(lane < HDIM, to_q[0], to_q[1]))
        out_ref[:, at_k] = low(to_k[0] + to_k[1])
        out_ref[:, at_v] = low(to_v[0] + to_v[1])
        return carry

    lax.fori_loop(0, width // 128, step, 0)


def attend(body, arrays, columns, score_scale):
    rows = arrays[0].shape[0]
    return pl.pallas_call(
        functools.partial(body, score_scale),
        grid=(rows // SEQ,),
        in_specs=[pl.BlockSpec((SEQ, array.shape[1]), lambda item: (item, 0)) for array in arrays],
        out_specs=pl.BlockSpec((SEQ, columns), lambda item: (item, 0)),
        out_shape=jax.ShapeDtypeStruct((rows, columns), jnp.bfloat16),
        cost_estimate=SMALL_COST,
    )(*arrays)


def condition_of(timesteps, labels, time_weight, time_bias, class_table):
    freq_emb = low(sinus_table(timesteps, time_weight.shape[0]))
    label_hot = low(
        labels[:, None] == jnp.arange(class_table.shape[0], dtype=jnp.int32)[None, :]
    )
    condition = mat_prod(freq_emb, time_weight) + time_bias + mat_prod(label_hot, class_table)
    return freq_emb, label_hot, condition, low(jax.nn.silu(condition))


def per_device(
    patches,
    cotangent,
    timesteps,
    labels,
    routes,
    slot_index,
    time_weight,
    time_bias,
    class_table,
    ada_weight,
    ada_bias,
    qkv_weight,
    proj_weight,
    router_weight,
    shared_in,
    shared_out,
    expert_in,
    expert_out,
):
    tokens, model_dim = patches.shape
    item_count = timesteps.shape[0]
    experts = lax.axis_size("exp")
    place_exp = lax.axis_index("exp")
    capacity = 9 * tokens // (4 * experts)
    slots_all = experts * capacity
    score_scale = 1.0 / math.sqrt(HDIM)

    own_in, own_out = expert_in[0], expert_out[0]
    far_mask = bits_of("hid")[-1]
    far_in = swap(own_in, "hid", far_mask)

    freq_emb, label_hot, condition, silu_cond = condition_of(
        timesteps, labels, time_weight, time_bias, class_table
    )
    modulate = mat_prod(silu_cond, ada_weight) + ada_bias
    shift_one, scale_one, gate_one, shift_two, scale_two, gate_two = [
        modulate[:, None, block_index * model_dim : (block_index + 1) * model_dim]
        for block_index in range(6)
    ]
    grad_result = cotangent.astype(jnp.float32).reshape(item_count, SEQ, model_dim)
    grad_branch = (gate_two * grad_result).reshape(tokens, model_dim)
    grad_branch_low = low(grad_branch)

    first_route, second_route = routes[:, 0:1], routes[:, 1:2]
    kept_first = slot_index[:, 0:1] < capacity
    kept_second = slot_index[:, 1:2] < capacity
    slot_ids = jnp.arange(slots_all, dtype=jnp.int32)[None, :]
    dispatch_first = low(
        (first_route * capacity + slot_index[:, 0:1] == slot_ids) & kept_first
    )
    dispatch_second = low(
        (second_route * capacity + slot_index[:, 1:2] == slot_ids) & kept_second
    )
    dispatch_both = dispatch_first + dispatch_second
    picks = jnp.concatenate([dispatch_first, dispatch_second], axis=0)
    grad_rows = exchange(low(prod_rows(dispatch_both, grad_branch_low)))
    grad_tokens, _ = gather_rows(grad_branch_low)

    residual = patches.astype(jnp.float32).reshape(item_count, SEQ, model_dim)
    normed_one, inverse_one = normalize(residual)
    flat_one = low(normed_one * (1.0 + scale_one) + shift_one).reshape(tokens, model_dim)
    qkv_rows = low(mat_prod(flat_one, qkv_weight))
    qkv_rows, far_in = lax.optimization_barrier((qkv_rows, far_in))
    attended_low = attend(attend_body, [qkv_rows], model_dim, score_scale)
    branch_one = mat_prod(attended_low, proj_weight).reshape(item_count, SEQ, model_dim)
    residual_one = residual + gate_one * branch_one
    normed_two, inverse_two = normalize(residual_one)
    hidden_two = low(normed_two * (1.0 + scale_two) + shift_two).reshape(tokens, model_dim)
    logits = mat_prod(hidden_two, router_weight)
    expert_ids = jnp.arange(experts, dtype=jnp.int32)[None, :]
    first_hot = (first_route == expert_ids).astype(jnp.float32)
    second_hot = (second_route == expert_ids).astype(jnp.float32)
    logit_gap = jnp.sum(logits * first_hot, axis=1) - jnp.sum(logits * second_hot, axis=1)
    gate_first = jax.nn.sigmoid(logit_gap)[:, None]
    gate_second = 1.0 - gate_first

    lane = jnp.arange(128, dtype=jnp.int32)[None, :]

    def gate_lanes(gate):
        high = low(gate).astype(jnp.float32)
        return low(jnp.where(lane == 0, high, jnp.where(lane == 1, gate - high, 0.0)))

    carried = jnp.concatenate(
        [
            jnp.concatenate([hidden_two, hidden_two], axis=0),
            jnp.concatenate([gate_lanes(gate_first), gate_lanes(gate_second)], axis=0),
        ],
        axis=1,
    )
    sent_rows, grad_rows = lax.optimization_barrier((low(prod_rows(picks, carried)), grad_rows))
    received = exchange(sent_rows)
    blocks_in = gather_hid(own_in, far_in)
    tokens_all, first_tokens = gather_rows(hidden_two)
    far_out = swap(after(own_out, first_tokens[:1, :128]), "hid", far_mask)
    blocks_out = gather_hid(own_out, far_out)

    halves = [
        expert_pass(rows, grads, [shared_in], [shared_out], False)
        for rows, grads in zip(tokens_all, grad_tokens)
    ]
    term_part, sum_part, act_shared, back_shared = zip(*halves)
    near_term, far_term = reduce_more(reduce_rows(term_part)[0])
    shared_term = near_term + far_term.astype(jnp.float32)
    weight_shared = shared_outer(*tokens_all, *grad_tokens, *act_shared, *back_shared)

    received, weight_shared = lax.optimization_barrier((received, weight_shared))
    share = model_dim // experts
    weight_shared = weight_shared.reshape(2, experts, share, weight_shared.shape[2])
    weight_shared = reduce_step(weight_shared, "exp", 0)
    grad_sent, expert_rows, grad_gated, *kept = expert_pass(
        received, grad_rows, blocks_in, blocks_out, True
    )
    grad_sent, sum_part, weight_shared = lax.optimization_barrier(
        (grad_sent, sum_part, weight_shared)
    )
    shared_sum, first_sum = reduce_rows(sum_part)
    grad_back = exchange(grad_sent)
    grad_gated, first_sum = lax.optimization_barrier((grad_gated, first_sum))
    blocks = list(range(len(blocks_in)))
    shares = {}
    for mask in bits_of("hid")[:-1]:
        here, there = [r for r in blocks if not r & mask], [r for r in blocks if r & mask]
        made = outer_pass(
            received,
            grad_gated,
            [kept[r] for r in there],
            [kept[len(blocks_in) + r] for r in there],
            added=[part for kind in range(2) for part in (shares[kind, r] for r in there)]
            if shares
            else (),
        )
        shares = {
            (kind, r): swap(made[kind][there.index(r | mask)], "hid", mask)
            for kind in range(2)
            for r in here
        }
        blocks = here
    made_in, made_out = outer_pass(
        received,
        grad_gated,
        [kept[r] for r in blocks],
        [kept[len(blocks_in) + r] for r in blocks],
        added=[shares[kind, r] for kind in range(2) for r in blocks],
    )
    (kept_in, sent_in), (kept_out, sent_out) = made_in, made_out
    near_sum, far_sum = reduce_more(shared_sum)
    grad_back, expert_rows, sent_in, sent_out, weight_shared, far_sum = lax.optimization_barrier(
        (grad_back, expert_rows, sent_in, sent_out, weight_shared, far_sum)
    )
    shared_sum = near_sum + far_sum.astype(jnp.float32)
    moved_in = swap(sent_in, "hid", far_mask)
    cut = sent_out.shape[0] // PIECES
    moved_out, last = [], moved_in
    for piece in range(PIECES):
        last, part = lax.optimization_barrier((last, sent_out[piece * cut : (piece + 1) * cut]))
        if piece == 0:
            moved_in = last
        else:
            moved_out[-1] = last
        last = swap(part, "hid", far_mask)
        moved_out.append(last)
    weight_shared = spread_rest(weight_shared)
    back_rows = exchange(expert_rows)

    picked_grad = mat_prod(picks, grad_back)
    dots = jnp.sum(picked_grad[:, model_dim:], axis=1)
    picked_grad = picked_grad[:, :model_dim]
    grad_gap = (dots[:tokens] - dots[tokens:])[:, None] * gate_first * gate_second
    grad_logits = low(grad_gap * (first_hot - second_hot))
    grad_hidden = (
        prod_cols(grad_logits, router_weight)
        + shared_term
        + gate_first * picked_grad[:tokens]
        + gate_second * picked_grad[tokens:]
    ).reshape(item_count, SEQ, model_dim)
    grad_shift_two = jnp.sum(grad_hidden, axis=1)
    grad_scale_two = jnp.sum(grad_hidden * normed_two, axis=1)
    grad_residual = grad_result + normalize_back(
        normed_two, inverse_two, grad_hidden * (1.0 + scale_two)
    )
    grad_gate_one = jnp.sum(branch_one * grad_residual, axis=1)
    grad_branch_one = low((gate_one * grad_residual).reshape(tokens, model_dim))
    grad_attended = low(prod_cols(grad_branch_one, proj_weight))
    moved_in, grad_attended = lax.optimization_barrier((moved_in, grad_attended))
    grad_qkv = attend(attend_back_body, [qkv_rows, grad_attended], 3 * model_dim, score_scale)
    back_rows, shared_sum, weight_shared, grad_qkv, first_out = lax.optimization_barrier(
        (back_rows, shared_sum, weight_shared, grad_qkv, moved_out[0])
    )
    moved_out = [first_out] + moved_out[1:]
    padded = jnp.pad(grad_logits, ((0, 0), (0, -experts % 128)))
    dense, (moved_out,) = sum_hid(
        jnp.concatenate(
            [
                low(prod_rows(flat_one, grad_qkv)),
                low(prod_rows(attended_low, grad_branch_one)),
                low(prod_rows(hidden_two, padded)),
            ],
            axis=1,
        ),
        (moved_out,),
    )
    tail = dense[:1, :128]
    moved_out = jnp.concatenate(moved_out, axis=0)
    weight_expert_in = kept_in.astype(jnp.float32) + after(moved_in, tail).astype(jnp.float32)
    weight_expert_out = kept_out.astype(jnp.float32) + after(moved_out, tail).astype(jnp.float32)
    weight_shared = sum(part.astype(jnp.float32) for part in weight_shared)
    grad_hidden_one = prod_cols(grad_qkv, qkv_weight).reshape(item_count, SEQ, model_dim)
    grad_shift_one = jnp.sum(grad_hidden_one, axis=1)
    grad_scale_one = jnp.sum(grad_hidden_one * normed_one, axis=1)
    grad_input = grad_residual + normalize_back(
        normed_one, inverse_one, grad_hidden_one * (1.0 + scale_one)
    )
    grad_patches = low(grad_input.reshape(tokens, model_dim))
    picked = mat_prod(picks, back_rows)
    picked_first, picked_second = picked[:tokens], picked[tokens:]
    moe_out = gate_first * picked_first + gate_second * picked_second
    branch_two = (shared_sum + moe_out).reshape(item_count, SEQ, model_dim)
    output = low(residual_one + gate_two * branch_two).reshape(tokens, model_dim)
    grad_gate_two = jnp.sum(branch_two * grad_result, axis=1)
    counts_local = jnp.sum(
        first_hot * kept_first.astype(jnp.float32) + second_hot * kept_second.astype(jnp.float32),
        axis=0,
    )
    counts_rows = jnp.where(jnp.arange(item_count)[:, None] == 0, counts_local[None, :], 0.0)
    digits = jnp.stack(
        [timesteps >> 5, timesteps & 31, labels >> 5, labels & 31], axis=1
    ).astype(jnp.float32)
    item_rows = low(
        jnp.concatenate(
            [
                grad_shift_one,
                grad_scale_one,
                grad_gate_one,
                grad_shift_two,
                grad_scale_two,
                grad_gate_two,
                digits,
                counts_rows,
                jnp.zeros((item_count, -(experts + 4) % 128), jnp.float32),
            ],
            axis=1,
        )
    )
    item_rows, dense = gather_items(item_rows, dense)
    dense = sum_parts(exchange(dense))

    grad_modulate = item_rows[:, : 6 * model_dim]
    rest = item_rows[:, 6 * model_dim :].astype(jnp.float32)
    expert_counts = jnp.sum(rest[:, 4 : 4 + experts], axis=0)
    numbers = rest[:, 0:4:2] * 32.0 + rest[:, 1:4:2]
    freq_all, label_all, condition_all, silu_all = condition_of(
        numbers[:, 0].astype(jnp.int32),
        numbers[:, 1].astype(jnp.int32),
        time_weight,
        time_bias,
        class_table,
    )
    weight_ada = prod_rows(
        lax.dynamic_slice_in_dim(silu_all, place_exp * share, share, 1), grad_modulate
    )
    bias_ada = jnp.sum(grad_modulate.astype(jnp.float32), axis=0)
    grad_silu = prod_cols(grad_modulate, ada_weight)
    grad_condition = jax.vjp(jax.nn.silu, condition_all)[1](grad_silu)[0]
    bias_time = jnp.sum(grad_condition, axis=0)
    grad_condition_low = low(grad_condition)
    table_grad = prod_rows(label_all, grad_condition_low)
    freq_share = time_weight.shape[0] // experts
    weight_time = prod_rows(
        lax.dynamic_slice_in_dim(freq_all, place_exp * freq_share, freq_share, 1),
        grad_condition_low,
    )
    return (
        output,
        grad_patches,
        weight_time,
        bias_time,
        table_grad,
        weight_ada,
        bias_ada,
        dense[:, : 3 * model_dim],
        dense[:, 3 * model_dim : 4 * model_dim],
        dense[:, 4 * model_dim : 4 * model_dim + experts],
        weight_shared[0],
        weight_shared[1].T,
        weight_expert_in[None],
        weight_expert_out[None],
        expert_counts,
    )


def solution(mesh):
    placed = (
        P(("exp", "hid"), None),
        P(("exp", "hid"), None),
        P(("exp", "hid")),
        P(("exp", "hid")),
        P(("exp", "hid"), None),
        P(("exp", "hid"), None),
        P(),
        P(),
        P(),
        P(),
        P(),
        P(),
        P(),
        P(),
        P(None, "hid"),
        P("hid", None),
        P("exp", None, "hid"),
        P("exp", "hid", None),
    )
    return jax.shard_map(
        per_device,
        mesh=mesh,
        in_specs=placed,
        out_specs=(
            P(("exp", "hid"), None),
            P(("exp", "hid"), None),
            P("exp", None),
            P(),
            P(),
            P("exp", None),
            P(),
            P("exp", None),
            P("exp", None),
            P("exp", None),
            P("exp", "hid"),
            P("hid", "exp"),
            P("exp", None, "hid"),
            P("exp", "hid", None),
            P(),
        ),
        check_vma=False,
    )
```
